128 devices in a mesh: dp: 4 (over z), expert: 32 (over x, y, core).
Axes of the slice: x: 4, y: 4, z: 4, core: 2. Of those that a mesh axis runs over, the one named last changes fastest.
Arguments:
- tokens: bfloat16 [4096, 3584], P('expert', 'dp'), may hold values from -6 to 6
- cotangent: bfloat16 [4096, 3584], P('expert', 'dp'), may hold values from -6 to 6
- routes: int32 [4096, 8], P('expert'), may hold values from 0 to 23, all different within a row; in each aligned block of 128 rows (0 to 127, 128 to 255, ...) at most 48 rows name the same one
- route_weight: float32 [4096, 8], P('expert'), may hold values from 0.1 to 0.6
- gate_weight: bfloat16 [32, 3584, 1024], P('expert', None, 'dp'), may hold values from -6 to 6
- up_weight: bfloat16 [32, 3584, 1024], P('expert', None, 'dp'), may hold values from -6 to 6
- down_weight: bfloat16 [32, 1024, 3584], P('expert', None, 'dp'), may hold values from -6 to 6
- first_moment: bfloat16 [32, 3584, 1024], P('expert', None, 'dp'), may hold values from -0.59765625 to 0.59765625
- second_moment: bfloat16 [32, 3584, 1024], P('expert', None, 'dp'), may hold values from 0.0009994507 to 0.029907227
- placement: int32 [32], replicated, may hold values from 0 to 23, as said below
- migration_plan: int32 [32], replicated, may hold values from 0 to 31, as said below
Outputs:
- layer_output: bfloat16 [4096, 3584], P('expert', 'dp')
- new_gate: bfloat16 [32, 3584, 1024], P('expert', None, 'dp')
- new_first: bfloat16 [32, 3584, 1024], P('expert', None, 'dp')
- new_second: bfloat16 [32, 3584, 1024], P('expert', None, 'dp')
The draws below stay inside these ranges and needn't reach their ends.
Inputs may be any that keep to these rules, and one draw needn't show every extreme that they name: `routes`: each row names 8 different experts; among the rows of one index of the expert axis no expert is named more than 48 times. `placement`: every expert from 0 to 23 is held by one slot or more. `migration_plan`: every expert keeps one slot or more in the new placement.
All inputs are finite; a program needn't handle non-finite values.
Results may differ from the reference program's by a relative error of at most 0.033.
Values may be sent and summed in bfloat16 or wider, within the bound.
No kernel may reach another device: no remote copies, remote signals or barrier semaphores. Data moves between devices by JAX's collectives and lax.ppermute only.
A program may use at most 128 MiB of HBM per device.

```python
import math
import jax
import jax.numpy as jnp
import numpy as np
from jax import lax

D = 3584
FF = 1024
TOK_DEV = 128
EXPERTS = 24
TOP = 8
CAP = 48
TOKENS = 4096
N_DP = 4
N_EXPERT = 32


def placement_tables(key):
    key_order, key_extra = jax.random.split(jax.random.fold_in(key, 11))
    order = jax.random.permutation(key_order, N_EXPERT).astype(jnp.int32)
    extra = jax.random.randint(key_extra, (N_EXPERT,), 0, EXPERTS).astype(jnp.int32)
    ranks = jnp.arange(N_EXPERT, dtype=jnp.int32)
    expert_of_rank = jnp.where(ranks < EXPERTS, ranks, extra)
    placement = jnp.zeros((N_EXPERT,), jnp.int32).at[order].set(expert_of_rank)
    rank_of_slot = jnp.argsort(order, stable=True).astype(jnp.int32)
    return (placement, order, rank_of_slot)


def draw_placement(key, part):
    return placement_tables(key)[0]


def draw_migration_plan(key, part):
    placement, order, rank_of_slot = placement_tables(key)
    key_base, key_coin, key_primary = jax.random.split(jax.random.fold_in(key, 23), 3)
    base = jax.random.permutation(key_base, N_EXPERT).astype(jnp.int32)
    is_extra = rank_of_slot[base] >= EXPERTS
    coin = jax.random.randint(key_coin, (N_EXPERT,), 0, 2) == 1
    primary = order[jax.random.randint(key_primary, (N_EXPERT,), 0, EXPERTS)]
    return jnp.where(is_extra & coin, primary, base).astype(jnp.int32)


def level_of(key, dims, cuts, low, largest):
    def one(dim, parts):
        draws = jax.random.uniform(jax.random.fold_in(jax.random.fold_in(key, 6), dim), (parts,), jnp.float32, low / len(cuts), largest / len(cuts))
        return jnp.repeat(jnp.exp(draws), dims[dim] // parts).reshape((-1,) + (1,) * (len(dims) - dim - 1))

    gain = one(*cuts[0])
    for cut in cuts[1:]:
        gain = gain * one(*cut)
    return gain


def deal_out(stream_key, own, number, rows, amount, top, most, skew):
    sequence = jax.random.permutation(stream_key, amount)
    heavy_load, common = portions_of(amount, rows * top, most, skew, True), portions_of(amount, rows * top, most, skew, False)
    places = jnp.arange(amount)

    def named(lengths, rotation):
        used = int((lengths > 0).sum())
        fixed = max(1, used // 4)
        shifted = fixed + (places - fixed + rotation * (used - fixed)) % max(1, amount - fixed)
        return jnp.zeros((amount,), jnp.int32).at[sequence[jnp.where(places < fixed, places, shifted)]].set(jnp.asarray(lengths, jnp.int32))

    lengths = jnp.where(number % 4 == 0, named(heavy_load, number // 4), named(common, number - number // 4 - 1))
    mixed = jax.random.permutation(jax.random.fold_in(own, 3), amount)
    source_of, taker = mixed[0:amount // 2 * 2:2], mixed[1:amount // 2 * 2:2]
    margin = jnp.minimum(lengths[source_of] - 1, most - lengths[taker]) // 2
    margin = jnp.where((source_of == sequence[0]) | (taker == sequence[0]) | (lengths[taker] == 0), 0, jnp.maximum(margin, 0))
    shifted = jax.random.randint(jax.random.fold_in(own, 4), (amount // 2,), 0, 1 << 20) % (margin + 1)
    lengths = lengths.at[source_of].add(-shifted).at[taker].add(shifted)
    labels = jnp.searchsorted(jnp.cumsum(lengths), jnp.arange(rows * top), side="right").astype(jnp.int32)
    grid = labels.reshape(top, rows).T
    grid = grid[jax.random.permutation(jax.random.fold_in(own, 1), rows)]
    rotation = jax.random.randint(jax.random.fold_in(own, 2), (rows, 1), 0, top)
    return jnp.take_along_axis(grid, (jnp.arange(top)[None, :] + rotation) % top, axis=1)


def portions_of(amount, total, bound, skew, full):
    portions = [(1 << 20) // math.isqrt(rank ** skew) + 1 for rank in range(1, amount + 1)]
    largest = bound if full else min(bound, max(-(-total // amount), total * portions[0] // sum(portions)))
    least = 1 if total - largest >= amount - 1 else 0
    counts, spare = [largest] + [least] * (amount - 1), total - largest - least * (amount - 1)
    while spare > 0:
        movable = [i for i in range(1, amount) if counts[i] < largest] or [i for i in range(1, amount) if counts[i] < bound]
        mass, budget = sum([portions[i] for i in movable]), spare
        for i in movable:
            more = min(bound - counts[i], max(1, budget * portions[i] // mass), spare)
            counts[i] = counts[i] + more
            spare = spare - more
    return np.array(counts)


def scatter_about(rng, shape, spread, most, cuts=(), held_as=jnp.bfloat16):
    factor_of = level_of(rng, shape, cuts, -0.22, 0.18) if cuts else 1.0
    array = jax.random.normal(rng, shape, jnp.float32) * spread * factor_of
    return jnp.minimum(jnp.maximum(array, -most), most).astype(held_as)


def setup_inputs(seed: int = 0) -> dict:
    seeds = jax.random.split(jax.random.key(seed), 12)
    tokens = scatter_about(seeds[0], (TOKENS, D), 1.0, 6.0, ((0, 32), (1, 4)))
    cotangent = scatter_about(seeds[1], (TOKENS, D), 1.0, 6.0, ((0, 32), (1, 4)))
    routes_keys = jax.random.split(jax.random.fold_in(seeds[2], 1), TOKENS // TOK_DEV)
    routes_turns = jax.random.permutation(jax.random.fold_in(seeds[2], 3), TOKENS // TOK_DEV)
    routes = jax.vmap(lambda own, number: deal_out(jax.random.fold_in(seeds[2], 2), own, number, TOK_DEV, EXPERTS, TOP, CAP, 2))(routes_keys, routes_turns).reshape((TOKENS, TOP))
    route_weight = jnp.clip(0.1 + 0.5 * jax.random.uniform(seeds[3], (TOKENS, TOP), jnp.float32) ** level_of(seeds[3], (TOKENS, TOP), ((0, 32),), -0.2, 0.2), 0.1, 0.6)
    gate_weight = scatter_about(seeds[4], (N_EXPERT, D, FF), 1.0, 6.0, ((0, 32), (2, 4)))
    up_weight = scatter_about(seeds[5], (N_EXPERT, D, FF), 1.0, 6.0, ((0, 32), (2, 4)))
    down_weight = scatter_about(seeds[6], (N_EXPERT, FF, D), 1.0, 6.0, ((0, 32), (2, 4)))
    first_moment = scatter_about(seeds[7], (N_EXPERT, D, FF), 0.1, 0.59765625, ((0, 32), (2, 4)))
    second_moment = jnp.clip(jnp.exp(math.log(0.029907227) - 3.3986496 * jax.random.uniform(seeds[8], (N_EXPERT, D, FF), jnp.float32) ** level_of(seeds[8], (N_EXPERT, D, FF), ((0, 32), (2, 4)), -0.2, 0.2)), 0.0009994507, 0.029907227).astype(jnp.bfloat16)
    placement = draw_placement(jax.random.fold_in(seeds[11], 71), 0)
    migration_plan = draw_migration_plan(jax.random.fold_in(seeds[11], 71), 0)
    return dict(tokens=tokens, cotangent=cotangent, routes=routes, route_weight=route_weight, gate_weight=gate_weight, up_weight=up_weight, down_weight=down_weight, first_moment=first_moment, second_moment=second_moment, placement=placement, migration_plan=migration_plan)


beta_first = 0.9
beta_second = 0.95
learn_rate = 0.02
weight_decay = 0.1
epsilon = 1e-08

def choose_slots(routes, placement, source):
    slot_iota = jnp.arange(placement.shape[0], dtype=jnp.int32)
    hosting = routes[..., None] == placement
    copies = lax.optimization_barrier(jnp.sum(hosting, -1)).astype(jnp.int32)
    earlier = (placement[:, None] == placement[None, :]) & (slot_iota[:, None] < slot_iota[None, :])
    replica_rank = lax.optimization_barrier(jnp.sum(earlier, 0)).astype(jnp.int32)
    replica = source[:, None] % copies
    matched = hosting & (replica_rank == replica[..., None])
    return lax.optimization_barrier(jnp.sum(jnp.where(matched, slot_iota, 0), -1)).astype(jnp.int32)

def place_rows(slot_ids, slot_count):
    tok_rows, per_token = slot_ids.shape
    flattened = slot_ids.reshape(-1)
    onehot = (flattened[:, None] == jnp.arange(slot_count, dtype=jnp.int32)).astype(jnp.int32)
    running = jnp.cumsum(onehot, 0)
    return (lax.optimization_barrier(jnp.sum(running * onehot, 1)) - 1).astype(jnp.int32).reshape(tok_rows, per_token)

def adam_update(gradient, weight, first_old, second):
    moment_one = beta_first * first_old.astype(jnp.float32) + (1.0 - beta_first) * gradient
    moment_two = beta_second * second.astype(jnp.float32) + (1.0 - beta_second) * gradient * gradient
    updated = weight.astype(jnp.float32) * (1.0 - learn_rate * weight_decay) - learn_rate * moment_one / (jnp.sqrt(moment_two) + epsilon)
    return (updated, moment_one, moment_two)

def reference(tokens, cotangent, routes, route_weight, gate_weight, up_weight, down_weight, first_moment, second_moment, placement, migration_plan):
    scale_in = 1.0 / math.sqrt(D)
    scale_mid = 1.0 / math.sqrt(FF)
    quarter = D // N_DP
    source = (jnp.arange(TOKENS, dtype=jnp.int32) // TOK_DEV).astype(jnp.int32)
    slot_ids = choose_slots(routes, placement, source)

    def block_rows(block):
        return place_rows(block, N_EXPERT)
    position = jax.vmap(block_rows)(slot_ids.reshape(N_EXPERT, TOK_DEV, TOP)).reshape(TOKENS, TOP)
    buffer_row = (source[:, None] * CAP + position).astype(jnp.int32)
    token_buffer = jnp.zeros((N_EXPERT, N_EXPERT * CAP, D), jnp.bfloat16)
    grad_buffer = jnp.zeros((N_EXPERT, N_EXPERT * CAP, D), jnp.bfloat16)
    for route_index in range(TOP):
        token_buffer = token_buffer.at[slot_ids[:, route_index], buffer_row[:, route_index]].set(tokens)
        scaled = (route_weight[:, route_index:route_index + 1] * cotangent.astype(jnp.float32)).astype(jnp.bfloat16)
        grad_buffer = grad_buffer.at[slot_ids[:, route_index], buffer_row[:, route_index]].set(scaled)

    def expert_step(operands):
        inputs, upstream, w_gate, w_up, w_down = operands
        gate_values = jnp.dot(inputs, w_gate, preferred_element_type=jnp.float32) * scale_in
        up_values = jnp.dot(inputs, w_up, preferred_element_type=jnp.float32) * scale_in
        hidden = (jax.nn.silu(gate_values) * up_values).astype(jnp.bfloat16)
        outputs = (jnp.dot(hidden, w_down, preferred_element_type=jnp.float32) * scale_mid).astype(jnp.bfloat16)
        hidden_grad = jnp.zeros(gate_values.shape, jnp.float32)
        for quarter_index in range(N_DP):
            lower = quarter_index * quarter
            partial_grad = jnp.dot(upstream[:, lower:lower + quarter], w_down[:, lower:lower + quarter].T, preferred_element_type=jnp.float32)
            hidden_grad = hidden_grad + partial_grad.astype(jnp.bfloat16).astype(jnp.float32)
        hidden_grad = hidden_grad * scale_mid
        sigmoid_gate = jax.nn.sigmoid(gate_values)
        gate_grad = (hidden_grad * up_values * sigmoid_gate * (1.0 + gate_values * (1.0 - sigmoid_gate))).astype(jnp.bfloat16)
        weight_grad = jnp.dot(inputs.T, gate_grad, preferred_element_type=jnp.float32) * scale_in
        return (outputs, weight_grad)
    expert_out, slot_grad = lax.map(expert_step, (token_buffer, grad_buffer, gate_weight, up_weight, down_weight))
    combined = jnp.zeros((TOKENS, D), jnp.float32)
    for route_index in range(TOP):
        rows_back = expert_out[slot_ids[:, route_index], buffer_row[:, route_index]].astype(jnp.float32)
        combined = combined + route_weight[:, route_index:route_index + 1] * rows_back
    layer_output = combined.astype(jnp.bfloat16)
    same_expert = (placement[:, None] == placement[None, :]).astype(jnp.float32)
    expert_grad = jnp.dot(same_expert, slot_grad.reshape(N_EXPERT, -1), precision=lax.Precision.HIGHEST).reshape(slot_grad.shape)
    updated, first, second = adam_update(expert_grad, gate_weight, first_moment, second_moment)
    new_gate = updated[migration_plan].astype(jnp.bfloat16)
    new_first = first[migration_plan].astype(jnp.bfloat16)
    new_second = second[migration_plan].astype(jnp.bfloat16)
    return (layer_output, new_gate, new_first, new_second)
```

```python
import functools
import math

import jax
import jax.numpy as jnp
from jax import lax
from jax.experimental import pallas as pl
from jax.experimental.pallas import tpu as pltpu
from jax.sharding import PartitionSpec as P

D = 3584
FF = 1024
N_DP = 4
SLOTS = 32
CAP = 48
TOK = 128
QD = D // N_DP
QF = FF // N_DP
PART = D // SLOTS
CHUNKS = ((0, 16), (16, 48))
BLOCK = 256

beta_first = 0.9
beta_second = 0.95
learn_rate = 0.02
weight_decay = 0.1
epsilon = 1e-08
scale_in = 1.0 / math.sqrt(D)
scale_mid = 1.0 / math.sqrt(FF)


f32 = jnp.float32
bf16 = jnp.bfloat16
VMEM = pltpu.VMEM
SMEM = pltpu.SMEM


def vspec():
    return pl.BlockSpec(memory_space=VMEM)


def sspec():
    return pl.BlockSpec(memory_space=SMEM)


def cost(flops, nbytes):
    return pl.CostEstimate(flops=flops, transcendentals=0, bytes_accessed=nbytes)


def select_kernel(index, place_row, place_col, routes, weights, tokens, *outs):
    rows_out, sel_out, selw_out = outs[: len(CHUNKS)], outs[len(CHUNKS)], outs[len(CHUNKS) + 1]
    me = index[0].astype(f32)
    col = place_col[...]
    same = (col == place_row[...]).astype(f32)
    a = lax.broadcasted_iota(jnp.int32, (SLOTS, SLOTS), 0)
    b = lax.broadcasted_iota(jnp.int32, (SLOTS, SLOTS), 1)
    copies = jnp.sum(same, axis=1, keepdims=True)
    rank = jnp.sum(jnp.where(b < a, same, 0.0), axis=1, keepdims=True)
    turn = me - copies * jnp.floor((me + 0.5) / copies)
    active = jnp.abs(rank - turn) < 0.5
    hit = jnp.zeros((SLOTS, TOK), f32)
    wt = jnp.zeros((SLOTS, TOK), f32)
    for k in range(routes.shape[0]):
        match = (routes[k : k + 1, :] == col) & active
        hit = hit + jnp.where(match, 1.0, 0.0)
        wt = wt + jnp.where(match, weights[k : k + 1, :], 0.0)
    t0 = lax.broadcasted_iota(jnp.int32, (TOK, TOK), 0)
    t1 = lax.broadcasted_iota(jnp.int32, (TOK, TOK), 1)
    before = jnp.where(t0 < t1, 1.0, 0.0).astype(bf16)
    pos = jnp.dot(hit.astype(bf16), before, preferred_element_type=f32)
    pos = jnp.where(hit > 0.5, pos, -1.0)
    base = 0
    for lo, hi in CHUNKS:
        c = hi - lo
        want = (lax.broadcasted_iota(jnp.int32, (c, TOK), 0) + lo).astype(f32)
        for j in range(SLOTS):
            chosen = jnp.abs(pos[j : j + 1, :] - want) < 0.5
            sel_out[base + j * c : base + (j + 1) * c, :] = jnp.where(chosen, 1.0, 0.0).astype(bf16)
            selw_out[base + j * c : base + (j + 1) * c, :] = jnp.where(chosen, wt[j : j + 1, :], 0.0)
        base += SLOTS * c
    base = 0
    for (lo, hi), out in zip(CHUNKS, rows_out):
        total = SLOTS * (hi - lo)
        for r in range(0, total, 512):
            sel = sel_out[base + r : base + r + 512, :]
            out[r : r + 512, :] = jnp.dot(sel, tokens[...], preferred_element_type=f32).astype(bf16)
        base += total


def select_rows(index, placement, routes, weights, tokens):
    rows = SLOTS * CAP
    return pl.pallas_call(
        select_kernel,
        out_shape=[jax.ShapeDtypeStruct((SLOTS * (hi - lo), QD), bf16) for lo, hi in CHUNKS]
        + [jax.ShapeDtypeStruct((rows, TOK), bf16), jax.ShapeDtypeStruct((rows, TOK), f32)],
        in_specs=[sspec()] + [vspec()] * 5,
        out_specs=[vspec()] * (len(CHUNKS) + 2),
        cost_estimate=cost(2 * rows * TOK * QD, 4 << 20),
        name="select_rows",
    )(index, placement[None, :], placement[:, None], routes.T, weights.T, tokens)


def scale_kernel(sel, selw, cot, out):
    for r in range(0, SLOTS * CAP, 512):
        w = jnp.sum(selw[r : r + 512, :], axis=1, keepdims=True)
        picked = jnp.dot(sel[r : r + 512, :], cot[...], preferred_element_type=f32)
        out[r : r + 512, :] = (w * picked).astype(bf16)


def scale_rows(sel, selw, cot):
    rows = SLOTS * CAP
    return pl.pallas_call(
        scale_kernel,
        out_shape=jax.ShapeDtypeStruct((rows, QD), bf16),
        in_specs=[vspec()] * 3,
        out_specs=vspec(),
        cost_estimate=cost(2 * rows * TOK * QD, 4 << 20),
        name="scale_rows",
    )(sel, selw, cot)


def row_block(width):
    return pl.BlockSpec((BLOCK, width), lambda i: (i, 0))


def half_blocks(width, half):
    return [
        pl.BlockSpec((BLOCK, width), lambda i: (jnp.minimum(i, half - 1), 0)),
        pl.BlockSpec((BLOCK, width), lambda i: (jnp.maximum(i - half, 0), 0)),
    ]


def whole(shape):
    return pl.BlockSpec(shape, lambda i: (0,) * len(shape))


def quarter_rows(ref, q, size):
    return ref[pl.ds(pl.multiple_of(q * size, size), size), :]


def hidden_kernel(half, dp, own, left, right, fa, fb, wg, wu, g_out, u_out, h_out):
    i = pl.program_id(0)
    me = dp[0]
    far = jnp.where(i < half, fa[...], fb[...])
    pieces = ((0, own[...]), (3, left[...]), (1, right[...]), (2, far))

    def product(w):
        total = None
        for shift, x in pieces:
            q = lax.rem(me + shift, N_DP)
            part = jnp.dot(x, quarter_rows(w, q, QD), preferred_element_type=f32)
            total = part if total is None else total + part
        return total * scale_in

    g = product(wg)
    u = product(wu)
    g_out[...] = g
    u_out[...] = u
    h_out[...] = (g / (1.0 + jnp.exp(-g)) * u).astype(bf16)


def hidden_of(dp, pieces, wg, wu):
    rows = pieces[0].shape[0]
    blocks = rows // BLOCK
    return pl.pallas_call(
        functools.partial(hidden_kernel, blocks // 2),
        grid=(blocks,),
        out_shape=[
            jax.ShapeDtypeStruct((rows, QF), f32),
            jax.ShapeDtypeStruct((rows, QF), f32),
            jax.ShapeDtypeStruct((rows, QF), bf16),
        ],
        in_specs=[sspec()]
        + [row_block(QD)] * 3
        + half_blocks(QD, blocks // 2)
        + [whole((D, QF)), whole((D, QF))],
        out_specs=[row_block(QF)] * 3,
        cost_estimate=cost(4 * rows * D * QF, rows * D * 2 + 8 * D * QF),
        name="hidden",
    )(dp, *pieces, wg, wu)


def partial_kernel(x, wd, out):
    for q in range(N_DP):
        out[q] = lax.dot_general(
            x[...],
            wd[q * QF : (q + 1) * QF, :],
            (((1,), (1,)), ((), ())),
            preferred_element_type=f32,
        ).astype(bf16)


def partial_grads(x, wd):
    rows = x.shape[0]
    return pl.pallas_call(
        partial_kernel,
        grid=(rows // BLOCK,),
        out_shape=jax.ShapeDtypeStruct((N_DP, rows, QF), bf16),
        in_specs=[row_block(QD), whole((FF, QD))],
        out_specs=pl.BlockSpec((N_DP, BLOCK, QF), lambda i: (0, i, 0)),
        cost_estimate=cost(2 * rows * QD * FF, 6 << 20),
        name="partial_grads",
    )(x, wd)


def weight_kernel(half, first, last, *refs):
    dp, hg, g_in, u_in, own, left, right, fa, fb = refs[:9]
    acc = refs[-1]
    out = refs[-2]
    i = pl.program_id(0)
    me = dp[0]

    @pl.when(i == 0)
    def _():
        if first:
            acc[...] = jnp.zeros_like(acc)
        else:
            acc[...] = refs[9][...]

    grad = (hg[0].astype(f32) + hg[1].astype(f32)) + (hg[2].astype(f32) + hg[3].astype(f32))
    grad = grad * scale_mid
    g = g_in[...]
    s = 1.0 / (1.0 + jnp.exp(-g))
    gg = (grad * u_in[...] * s * (1.0 + g * (1.0 - s))).astype(bf16)
    far = jnp.where(i < half, fa[...], fb[...])
    for shift, x in ((0, own[...]), (3, left[...]), (1, right[...]), (2, far)):
        q = lax.rem(me + shift, N_DP)
        at = pl.ds(pl.multiple_of(q * QD, QD), QD)
        acc[:, at] += lax.dot_general(
            gg, x, (((0,), (0,)), ((), ())), preferred_element_type=f32
        )

    @pl.when(i == pl.num_programs(0) - 1)
    def _():
        if last:
            for r in range(0, D, 512):
                out[r : r + 512, :] = (acc[:, r : r + 512] * scale_in).T.astype(bf16)
        else:
            out[...] = acc[...]


def weight_grads(dp, hg, g, u, pieces, carry, last):
    rows = g.shape[0]
    blocks = rows // BLOCK
    first = carry is None
    shape = jax.ShapeDtypeStruct((D, QF), bf16) if last else jax.ShapeDtypeStruct((QF, D), f32)
    return pl.pallas_call(
        functools.partial(weight_kernel, blocks // 2, first, last),
        grid=(blocks,),
        out_shape=shape,
        in_specs=[sspec(), pl.BlockSpec((N_DP, BLOCK, QF), lambda i: (0, i, 0))]
        + [row_block(QF)] * 2
        + [row_block(QD)] * 3
        + half_blocks(QD, blocks // 2)
        + ([] if first else [whole((QF, D))]),
        out_specs=whole(shape.shape),
        scratch_shapes=[VMEM((QF, D), f32)],
        cost_estimate=cost(2 * rows * D * QF, rows * D * 2 + (8 << 20)),
        name="weight_grads",
    )(dp, hg, g, u, *pieces, *(() if first else (carry,)))


def output_kernel(half, dp, own, left, right, fa, fb, wd, out):
    i = pl.program_id(0)
    me = dp[0]
    far = jnp.where(i < half, fa[...], fb[...])
    total = None
    for shift, x in ((0, own[...]), (3, left[...]), (1, right[...]), (2, far)):
        q = lax.rem(me + shift, N_DP)
        part = jnp.dot(x, quarter_rows(wd, q, QF), preferred_element_type=f32)
        total = part if total is None else total + part
    out[...] = (total * scale_mid).astype(bf16)


def outputs_of(dp, pieces, wd):
    rows = pieces[0].shape[0]
    blocks = rows // BLOCK
    return pl.pallas_call(
        functools.partial(output_kernel, blocks // 2),
        grid=(blocks,),
        out_shape=jax.ShapeDtypeStruct((rows, QD), bf16),
        in_specs=[sspec()] + [row_block(QF)] * 3 + half_blocks(QF, blocks // 2) + [whole((FF, QD))],
        out_specs=row_block(QD),
        cost_estimate=cost(2 * rows * FF * QD, rows * (FF + QD) * 2),
        name="outputs",
    )(dp, *pieces, wd)


def combine_kernel(selw, *refs):
    out = refs[-1]
    total = jnp.zeros(out.shape, f32)
    base = 0
    for ref in refs[:-1]:
        n = ref.shape[0]
        w = selw[base : base + n, :]
        high = w.astype(bf16)
        low = (w - high.astype(f32)).astype(bf16)
        rows = ref[...]
        for part in (high, low):
            total = total + lax.dot_general(
                part, rows, (((0,), (0,)), ((), ())), preferred_element_type=f32
            )
        base += n
    out[...] = total.astype(bf16)


def combine(selw, rows):
    return pl.pallas_call(
        combine_kernel,
        out_shape=jax.ShapeDtypeStruct((TOK, QD), bf16),
        in_specs=[vspec()] * (1 + len(rows)),
        out_specs=vspec(),
        cost_estimate=cost(4 * SLOTS * CAP * TOK * QD, 4 << 20),
        name="combine",
    )(selw, *rows)


def migrate_kernel(plan, x, out):
    out[...] = x[...]


def migrate(plan, parts):
    return pl.pallas_call(
        migrate_kernel,
        grid_spec=pltpu.PrefetchScalarGridSpec(
            num_scalar_prefetch=1,
            grid=(SLOTS,),
            in_specs=[pl.BlockSpec((1, PART, QF), lambda s, plan: (plan[s], 0, 0))],
            out_specs=pl.BlockSpec((1, PART, QF), lambda s, plan: (s, 0, 0)),
        ),
        out_shape=jax.ShapeDtypeStruct((SLOTS, PART, QF), bf16),
        cost_estimate=cost(0, 4 << 20),
        name="migrate",
    )(plan, parts)


UPDATE_ROWS = 16


def update_kernel(plan, placement, grads, first, second, out, total):
    total[...] = jnp.zeros_like(total)
    for s in range(SLOTS):
        total[placement[s]] += grads[s].astype(f32)

    def body(s, carry):
        p = plan[s]
        g = total[placement[p]]
        one = beta_first * first[p].astype(f32) + (1.0 - beta_first) * g
        two = beta_second * second[p].astype(f32) + (1.0 - beta_second) * g * g
        out[s, 0] = one.astype(bf16)
        out[s, 1] = two.astype(bf16)
        return carry

    lax.fori_loop(0, SLOTS, body, 0, unroll=4)


def update(plan, placement, grads, first, second):
    part = pl.BlockSpec((SLOTS, UPDATE_ROWS, QF), lambda i, *_: (0, i, 0))
    return pl.pallas_call(
        update_kernel,
        grid_spec=pltpu.PrefetchScalarGridSpec(
            num_scalar_prefetch=2,
            grid=(PART // UPDATE_ROWS,),
            in_specs=[part] * 3,
            out_specs=pl.BlockSpec((SLOTS, 2, UPDATE_ROWS, QF), lambda i, *_: (0, 0, i, 0)),
            scratch_shapes=[VMEM((SLOTS, UPDATE_ROWS, QF), f32)],
        ),
        out_shape=jax.ShapeDtypeStruct((SLOTS, 2, PART, QF), bf16),
        cost_estimate=cost(20 * D * SLOTS * QF // SLOTS, 10 << 20),
        name="update",
    )(plan, placement, grads, first, second)


def finish_kernel(gate, moments, g_out, one_out, two_out):
    one = moments[:, 0]
    two = moments[:, 1]
    one_out[...] = one
    two_out[...] = two
    w = gate[...].astype(f32) * (1.0 - learn_rate * weight_decay)
    step = learn_rate * one.astype(f32) / (jnp.sqrt(two.astype(f32)) + epsilon)
    g_out[...] = (w - step).astype(bf16)


def finish(gate, moments):
    n = 4
    part = pl.BlockSpec((n, PART, QF), lambda i: (i, 0, 0))
    return pl.pallas_call(
        finish_kernel,
        grid=(SLOTS // n,),
        out_shape=[jax.ShapeDtypeStruct((SLOTS, PART, QF), bf16)] * 3,
        in_specs=[part, pl.BlockSpec((n, 2, PART, QF), lambda i: (i, 0, 0, 0))],
        out_specs=[part] * 3,
        cost_estimate=cost(20 * D * QF, 12 << 20),
        name="finish",
    )(gate, moments)


def exchange(x, axis="expert"):
    return lax.all_to_all(x, axis, split_axis=0, concat_axis=0, tiled=True)


FORWARD = [(i, (i + 1) % N_DP) for i in range(N_DP)]
BACKWARD = [(i, (i - 1) % N_DP) for i in range(N_DP)]


def ring(x):
    half = x.shape[0] // 2
    left = lax.ppermute(x, "dp", FORWARD)
    right = lax.ppermute(x, "dp", BACKWARD)
    fa = lax.ppermute(left[:half], "dp", FORWARD)
    fb = lax.ppermute(right[half:], "dp", BACKWARD)
    return (x, left, right, fa, fb)


def per_device(
    tokens,
    cotangent,
    routes,
    route_weight,
    gate_weight,
    up_weight,
    down_weight,
    first_moment,
    second_moment,
    placement,
    migration_plan,
):
    index = lax.axis_index("expert").astype(jnp.int32)[None]
    dp = lax.axis_index("dp").astype(jnp.int32)[None]
    wg, wu, wd = gate_weight[0], up_weight[0], down_weight[0]
    picked = select_rows(index, placement, routes, route_weight, tokens)
    sent, sel, selw = picked[: len(CHUNKS)], picked[-2], picked[-1]
    got = [
        exchange(x.reshape(SLOTS, -1, QD)).reshape(-1, QD) for x in sent
    ]
    sent_grads = scale_rows(sel, selw, cotangent)
    grads = []
    base = 0
    for lo, hi in CHUNKS:
        n = SLOTS * (hi - lo)
        grads.append(
            exchange(sent_grads[base : base + n].reshape(SLOTS, hi - lo, QD)).reshape(n, QD)
        )
        base += n
    parts = [
        exchange(x[0].reshape(SLOTS, PART, QF)) for x in (gate_weight, first_moment, second_moment)
    ]
    new_gate_in = exchange(migrate(migration_plan, parts[0]))
    carry = None
    hiddens = []
    for n in range(len(CHUNKS)):
        pieces = ring(got[n])
        g, u, h = hidden_of(dp, pieces, wg, wu)
        hg = exchange(partial_grads(grads[n], wd), "dp")
        carry = weight_grads(dp, hg, g, u, pieces, carry, n == len(CHUNKS) - 1)
        hiddens.append(h)
    got_wgrad = exchange(carry.reshape(SLOTS, PART, QF))
    moments = exchange(update(migration_plan, placement, got_wgrad, parts[1], parts[2]))
    returned = []
    for (lo, hi), h in zip(CHUNKS, hiddens):
        out = outputs_of(dp, ring(h), wd)
        returned.append(exchange(out.reshape(SLOTS, hi - lo, QD)).reshape(-1, QD))
    layer_output = combine(selw, returned)
    results = finish(new_gate_in, moments)
    return (layer_output,) + tuple(r.reshape(1, D, QF) for r in results)


def solution(mesh):
    placed = (
        P("expert", "dp"),
        P("expert", "dp"),
        P("expert", None),
        P("expert", None),
        P("expert", None, "dp"),
        P("expert", None, "dp"),
        P("expert", None, "dp"),
        P("expert", None, "dp"),
        P("expert", None, "dp"),
        P(),
        P(),
    )
    return jax.shard_map(
        per_device,
        mesh=mesh,
        in_specs=placed,
        out_specs=(
            P("expert", "dp"),
            P("expert", None, "dp"),
            P("expert", None, "dp"),
            P("expert", None, "dp"),
        ),
        check_vma=False,
    )
```

```python
import math

import jax
import jax.numpy as jnp
from jax import lax
from jax.experimental import pallas as pl
from jax.experimental.pallas import tpu as pltpu
from jax.sharding import PartitionSpec as P


D = 3584
FF = 1024
N_DP = 4
SLOTS = 32
CAP = 48
TOK = 128
QD = D // N_DP
QF = FF // N_DP
PART = D // SLOTS
CHUNKS = ((0, 48),)
ROWS = SLOTS * CAP
HALF = ROWS // 2

beta_first = 0.9
beta_second = 0.95
learn_rate = 0.02
weight_decay = 0.1
epsilon = 1e-08
scale_in = 1.0 / math.sqrt(D)
scale_mid = 1.0 / math.sqrt(FF)


f32 = jnp.float32
bf16 = jnp.bfloat16
VMEM = pltpu.VMEM
SMEM = pltpu.SMEM


def vspec():
    return pl.BlockSpec(memory_space=VMEM)


def sspec():
    return pl.BlockSpec(memory_space=SMEM)


def cost(flops, nbytes):
    return pl.CostEstimate(flops=flops, transcendentals=0, bytes_accessed=nbytes)


def select_kernel(index, place_row, place_col, routes, weights, tokens, *outs):
    rows_out, sel_out, selw_out = outs[: len(CHUNKS)], outs[len(CHUNKS)], outs[len(CHUNKS) + 1]
    me = index[0].astype(f32)
    col = place_col[...]
    same = (col == place_row[...]).astype(f32)
    a = lax.broadcasted_iota(jnp.int32, (SLOTS, SLOTS), 0)
    b = lax.broadcasted_iota(jnp.int32, (SLOTS, SLOTS), 1)
    copies = jnp.sum(same, axis=1, keepdims=True)
    rank = jnp.sum(jnp.where(b < a, same, 0.0), axis=1, keepdims=True)
    turn = me - copies * jnp.floor((me + 0.5) / copies)
    active = jnp.abs(rank - turn) < 0.5
    hit = jnp.zeros((SLOTS, TOK), f32)
    wt = jnp.zeros((SLOTS, TOK), f32)
    for k in range(routes.shape[0]):
        match = (routes[k : k + 1, :] == col) & active
        hit = hit + jnp.where(match, 1.0, 0.0)
        wt = wt + jnp.where(match, weights[k : k + 1, :], 0.0)
    t0 = lax.broadcasted_iota(jnp.int32, (TOK, TOK), 0)
    t1 = lax.broadcasted_iota(jnp.int32, (TOK, TOK), 1)
    before = jnp.where(t0 < t1, 1.0, 0.0).astype(bf16)
    pos = jnp.dot(hit.astype(bf16), before, preferred_element_type=f32)
    pos = jnp.where(hit > 0.5, pos, -1.0)
    base = 0
    for lo, hi in CHUNKS:
        c = hi - lo
        want = (lax.broadcasted_iota(jnp.int32, (c, TOK), 0) + lo).astype(f32)
        for j in range(SLOTS):
            chosen = jnp.abs(pos[j : j + 1, :] - want) < 0.5
            sel_out[base + j * c : base + (j + 1) * c, :] = jnp.where(chosen, 1.0, 0.0).astype(bf16)
            selw_out[base + j * c : base + (j + 1) * c, :] = jnp.where(chosen, wt[j : j + 1, :], 0.0)
        base += SLOTS * c
    base = 0
    for (lo, hi), out in zip(CHUNKS, rows_out):
        total = SLOTS * (hi - lo)
        for r in range(0, total, 512):
            sel = sel_out[base + r : base + r + 512, :]
            out[r : r + 512, :] = jnp.dot(sel, tokens[...], preferred_element_type=f32).astype(bf16)
        base += total


def select_rows(index, placement, routes, weights, tokens):
    rows = SLOTS * CAP
    return pl.pallas_call(
        select_kernel,
        out_shape=[jax.ShapeDtypeStruct((SLOTS * (hi - lo), QD), bf16) for lo, hi in CHUNKS]
        + [jax.ShapeDtypeStruct((rows, TOK), bf16), jax.ShapeDtypeStruct((rows, TOK), f32)],
        in_specs=[sspec()] + [vspec()] * 5,
        out_specs=[vspec()] * (len(CHUNKS) + 2),
        cost_estimate=cost(2 * rows * TOK * QD, 4 << 20),
        name="select_rows",
    )(index, placement[None, :], placement[:, None], routes.T, weights.T, tokens)


def scale_kernel(sel, selw, cot, out):
    for r in range(0, SLOTS * CAP, 512):
        w = jnp.sum(selw[r : r + 512, :], axis=1, keepdims=True)
        picked = jnp.dot(sel[r : r + 512, :], cot[...], preferred_element_type=f32)
        out[r : r + 512, :] = (w * picked).astype(bf16)


def scale_rows(sel, selw, cot):
    rows = SLOTS * CAP
    return pl.pallas_call(
        scale_kernel,
        out_shape=jax.ShapeDtypeStruct((rows, QD), bf16),
        in_specs=[vspec()] * 3,
        out_specs=vspec(),
        cost_estimate=cost(2 * rows * TOK * QD, 4 << 20),
        name="scale_rows",
    )(sel, selw, cot)


def row_block(block, width):
    return pl.BlockSpec((block, width), lambda i: (i, 0))


def piece_specs(block, width):
    half = HALF // block
    low = pl.BlockSpec((block, width), lambda i: (jnp.minimum(i, half - 1), 0))
    high = pl.BlockSpec((block, width), lambda i: (jnp.maximum(i - half, 0), 0))
    return [row_block(block, width)] + [low, high] * 3


def whole(shape):
    return pl.BlockSpec(shape, lambda i: (0,) * len(shape))


def gather_pieces(block, dp, pieces, out):
    width = pieces[0].shape[1]
    first = pl.program_id(0) < HALF // block
    own, la, lb, ra, rb, fa, fb = pieces
    for shift, x in (
        (0, own[...]),
        (3, jnp.where(first, la[...], lb[...])),
        (1, jnp.where(first, ra[...], rb[...])),
        (2, jnp.where(first, fa[...], fb[...])),
    ):
        q = lax.rem(dp[0] + shift, N_DP)
        out[:, pl.ds(pl.multiple_of(q * width, width), width)] = x


HIDDEN_BLOCK = 384


def hidden_kernel(dp, *refs):
    pieces, (wg, wu, g_out, u_out, h_out, x) = refs[:7], refs[7:]
    gather_pieces(HIDDEN_BLOCK, dp, pieces, x)
    g = jnp.dot(x[...], wg[...], preferred_element_type=f32) * scale_in
    u = jnp.dot(x[...], wu[...], preferred_element_type=f32) * scale_in
    g_out[...] = g
    u_out[...] = u
    h_out[...] = (g / (1.0 + jnp.exp(-g)) * u).astype(bf16)


def hidden_of(dp, pieces, wg, wu):
    block = HIDDEN_BLOCK
    return pl.pallas_call(
        hidden_kernel,
        grid=(ROWS // block,),
        out_shape=[
            jax.ShapeDtypeStruct((ROWS, QF), f32),
            jax.ShapeDtypeStruct((ROWS, QF), f32),
            jax.ShapeDtypeStruct((ROWS, QF), bf16),
        ],
        in_specs=[sspec()] + piece_specs(block, QD) + [whole((D, QF)), whole((D, QF))],
        out_specs=[row_block(block, QF)] * 3,
        scratch_shapes=[VMEM((block, D), bf16)],
        cost_estimate=cost(4 * ROWS * D * QF, ROWS * D * 2 + 8 * D * QF),
        name="hidden",
    )(dp, *pieces, wg, wu)


PARTIAL_BLOCK = 384


def partial_kernel(dp, x, wd, *outs):
    for k, out in enumerate(outs):
        q = lax.rem(dp[0] + k, N_DP)
        out[...] = lax.dot_general(
            x[...],
            wd[pl.ds(pl.multiple_of(q * QF, QF), QF), :],
            (((1,), (1,)), ((), ())),
            preferred_element_type=f32,
        ).astype(bf16)


def partial_grads(dp, x, wd):
    block = PARTIAL_BLOCK
    return pl.pallas_call(
        partial_kernel,
        grid=(ROWS // block,),
        out_shape=[jax.ShapeDtypeStruct((ROWS, QF), bf16)] * N_DP,
        in_specs=[sspec(), row_block(block, QD), whole((FF, QD))],
        out_specs=[row_block(block, QF)] * N_DP,
        cost_estimate=cost(2 * ROWS * QD * FF, 6 << 20),
        name="partial_grads",
    )(dp, x, wd)


WEIGHT_BLOCK = 768


def weight_kernel(dp, h0, h1, h2, h3, g_in, u_in, *refs):
    pieces, (out, x, acc) = refs[:7], refs[7:]
    i = pl.program_id(0)
    gather_pieces(WEIGHT_BLOCK, dp, pieces, x)
    grad = h0[...].astype(f32) + h1[...].astype(f32) + h2[...].astype(f32) + h3[...].astype(f32)
    grad = grad * scale_mid
    g = g_in[...]
    s = 1.0 / (1.0 + jnp.exp(-g))
    gg = (grad * u_in[...] * s * (1.0 + g * (1.0 - s))).astype(bf16)
    part = lax.dot_general(gg, x[...], (((0,), (0,)), ((), ())), preferred_element_type=f32)

    @pl.when(i == 0)
    def _():
        acc[...] = part

    @pl.when(i == pl.num_programs(0) - 1)
    def _():
        for r in range(0, D, 512):
            total = (acc[:, r : r + 512] + part[:, r : r + 512]) * scale_in
            out[r : r + 512, :] = total.T.astype(bf16)


def weight_grads(dp, hg, g, u, pieces):
    block = WEIGHT_BLOCK
    assert ROWS // block == 2
    return pl.pallas_call(
        weight_kernel,
        grid=(ROWS // block,),
        out_shape=jax.ShapeDtypeStruct((D, QF), bf16),
        in_specs=[sspec()] + [row_block(block, QF)] * 6 + piece_specs(block, QD),
        out_specs=whole((D, QF)),
        scratch_shapes=[VMEM((block, D), bf16), VMEM((QF, D), f32)],
        cost_estimate=cost(2 * ROWS * D * QF, ROWS * D * 2 + (8 << 20)),
        name="weight_grads",
    )(dp, *hg, g, u, *pieces)


OUTPUT_BLOCK = 384


def output_kernel(dp, *refs):
    pieces, (wd, out, x) = refs[:7], refs[7:]
    gather_pieces(OUTPUT_BLOCK, dp, pieces, x)
    total = jnp.dot(x[...], wd[...], preferred_element_type=f32)
    out[...] = (total * scale_mid).astype(bf16)


def outputs_of(dp, pieces, wd):
    block = OUTPUT_BLOCK
    return pl.pallas_call(
        output_kernel,
        grid=(ROWS // block,),
        out_shape=jax.ShapeDtypeStruct((ROWS, QD), bf16),
        in_specs=[sspec()] + piece_specs(block, QF) + [whole((FF, QD))],
        out_specs=row_block(block, QD),
        scratch_shapes=[VMEM((block, FF), bf16)],
        cost_estimate=cost(2 * ROWS * FF * QD, ROWS * (FF + QD) * 2),
        name="outputs",
    )(dp, *pieces, wd)


def combine_kernel(selw, *refs):
    out = refs[-1]
    total = jnp.zeros(out.shape, f32)
    base = 0
    for ref in refs[:-1]:
        n = ref.shape[0]
        w = selw[base : base + n, :]
        high = w.astype(bf16)
        low = (w - high.astype(f32)).astype(bf16)
        rows = ref[...]
        for part in (high, low):
            total = total + lax.dot_general(
                part, rows, (((0,), (0,)), ((), ())), preferred_element_type=f32
            )
        base += n
    out[...] = total.astype(bf16)


def combine(selw, rows):
    return pl.pallas_call(
        combine_kernel,
        out_shape=jax.ShapeDtypeStruct((TOK, QD), bf16),
        in_specs=[vspec()] * (1 + len(rows)),
        out_specs=vspec(),
        cost_estimate=cost(4 * SLOTS * CAP * TOK * QD, 4 << 20),
        name="combine",
    )(selw, *rows)


def migrate_kernel(plan, x, out):
    for s in range(SLOTS):
        out[s] = x[plan[s]]


def migrate(plan, states):
    return pl.pallas_call(
        migrate_kernel,
        grid_spec=pltpu.PrefetchScalarGridSpec(
            num_scalar_prefetch=1,
            grid=(1,),
            in_specs=[pl.BlockSpec((SLOTS, PART, QF), lambda i, *_: (0, 0, 0))],
            out_specs=pl.BlockSpec((SLOTS, PART, QF), lambda i, *_: (0, 0, 0)),
        ),
        out_shape=jax.ShapeDtypeStruct((SLOTS, PART, QF), bf16),
        cost_estimate=cost(0, 4 << 20),
        name="migrate",
    )(plan, states)


UPDATE_ROWS = 16


def update_kernel(plan, placement, grads, first, second, out, total):
    total[...] = jnp.zeros_like(total)
    for s in range(SLOTS):
        total[placement[s]] += grads[s].astype(f32)

    def body(s, carry):
        p = plan[s]
        g = total[placement[p]]
        one = beta_first * first[p].astype(f32) + (1.0 - beta_first) * g
        two = beta_second * second[p].astype(f32) + (1.0 - beta_second) * g * g
        out[s, 0] = one.astype(bf16)
        out[s, 1] = two.astype(bf16)
        return carry

    lax.fori_loop(0, SLOTS, body, 0, unroll=4)


def update(plan, placement, grads, states):
    steps = PART // UPDATE_ROWS

    def part(n):
        return pl.BlockSpec((SLOTS, UPDATE_ROWS, QF), lambda i, *_: (0, n * steps + i, 0))

    return pl.pallas_call(
        update_kernel,
        grid_spec=pltpu.PrefetchScalarGridSpec(
            num_scalar_prefetch=2,
            grid=(steps,),
            in_specs=[part(0), part(1), part(2)],
            out_specs=pl.BlockSpec((SLOTS, 2, UPDATE_ROWS, QF), lambda i, *_: (0, 0, i, 0)),
            scratch_shapes=[VMEM((SLOTS, UPDATE_ROWS, QF), f32)],
        ),
        out_shape=jax.ShapeDtypeStruct((SLOTS, 2, PART, QF), bf16),
        cost_estimate=cost(20 * D * SLOTS * QF // SLOTS, 10 << 20),
        name="update",
    )(plan, placement, grads, states, states)


def finish_kernel(gate, moments, g_out, one_out, two_out):
    one = moments[:, 0]
    two = moments[:, 1]
    one_out[...] = one
    two_out[...] = two
    w = gate[...].astype(f32) * (1.0 - learn_rate * weight_decay)
    step = learn_rate * one.astype(f32) / (jnp.sqrt(two.astype(f32)) + epsilon)
    g_out[...] = (w - step).astype(bf16)


def finish(gate, moments):
    n = 4
    part = pl.BlockSpec((n, PART, QF), lambda i: (i, 0, 0))
    return pl.pallas_call(
        finish_kernel,
        grid=(SLOTS // n,),
        out_shape=[jax.ShapeDtypeStruct((SLOTS, PART, QF), bf16)] * 3,
        in_specs=[part, pl.BlockSpec((n, 2, PART, QF), lambda i: (i, 0, 0, 0))],
        out_specs=[part] * 3,
        cost_estimate=cost(20 * D * QF, 12 << 20),
        name="finish",
    )(gate, moments)


def exchange(x):
    return lax.all_to_all(x, "expert", split_axis=0, concat_axis=0, tiled=True)


def shift(x, by):
    return lax.ppermute(x, "dp", [(i, (i + by) % N_DP) for i in range(N_DP)])


def ring(x):
    low, high = x[:HALF], x[HALF:]
    la = shift(low, 1)
    rb = shift(high, -1)
    lb = shift(high, 1)
    ra = shift(low, -1)
    fa = shift(la, 1)
    fb = shift(rb, -1)
    return (x, la, lb, ra, rb, fa, fb)


def device_step(
    tokens,
    cotangent,
    routes,
    route_weight,
    gate_weight,
    up_weight,
    down_weight,
    first_moment,
    second_moment,
    placement,
    migration_plan,
):
    index = lax.axis_index("expert").astype(jnp.int32)[None]
    dp = lax.axis_index("dp").astype(jnp.int32)[None]
    wg, wu, wd = gate_weight[0], up_weight[0], down_weight[0]
    rows, sel, selw = select_rows(index, placement, routes, route_weight, tokens)
    got = exchange(rows.reshape(SLOTS, CAP, QD)).reshape(ROWS, QD)
    sent_grads = scale_rows(sel, selw, cotangent)
    got_grads = exchange(sent_grads.reshape(SLOTS, CAP, QD)).reshape(ROWS, QD)
    packed = jnp.concatenate(
        [x[0].reshape(SLOTS, PART, QF) for x in (gate_weight, first_moment, second_moment)],
        axis=1,
    )
    states = exchange(packed)
    new_gate_in = exchange(migrate(migration_plan, states))
    pieces = ring(got)
    g, u, h = hidden_of(dp, pieces, wg, wu)
    partials = partial_grads(dp, got_grads, wd)
    hg = [partials[0]] + [shift(partials[k], k) for k in range(1, N_DP)]
    wgrad = weight_grads(dp, hg, g, u, pieces)
    got_wgrad = exchange(wgrad.reshape(SLOTS, PART, QF))
    moments = exchange(update(migration_plan, placement, got_wgrad, states))
    out = outputs_of(dp, ring(h), wd)
    returned = exchange(out.reshape(SLOTS, CAP, QD)).reshape(ROWS, QD)
    layer_output = combine(selw, [returned])
    results = finish(new_gate_in, moments)
    return (layer_output,) + tuple(r.reshape(1, D, QF) for r in results)


def solution(mesh):
    placed = (
        P("expert", "dp"),
        P("expert", "dp"),
        P("expert", None),
        P("expert", None),
        P("expert", None, "dp"),
        P("expert", None, "dp"),
        P("expert", None, "dp"),
        P("expert", None, "dp"),
        P("expert", None, "dp"),
        P(),
        P(),
    )
    return jax.shard_map(
        device_step,
        mesh=mesh,
        in_specs=placed,
        out_specs=(
            P("expert", "dp"),
            P("expert", None, "dp"),
            P("expert", None, "dp"),
            P("expert", None, "dp"),
        ),
        check_vma=False,
    )
```

```python
import functools
import math

import jax
import jax.numpy as jnp
from jax import lax
from jax.experimental import pallas as pl
from jax.experimental.pallas import tpu as pltpu
from jax.sharding import PartitionSpec as P


D = 3584
FF = 1024
N_DP = 4
SLOTS = 32
CAP = 48
TOK = 128
QD = D // N_DP
QF = FF // N_DP
PART = D // SLOTS
CHUNKS = ((0, 16), (16, 48))
ROWS = SLOTS * CAP
HALF = SLOTS // 2

beta_first = 0.9
beta_second = 0.95
learn_rate = 0.02
weight_decay = 0.1
epsilon = 1e-08
scale_in = 1.0 / math.sqrt(D)
scale_mid = 1.0 / math.sqrt(FF)


f32 = jnp.float32
bf16 = jnp.bfloat16
VMEM = pltpu.VMEM
SMEM = pltpu.SMEM


def vspec():
    return pl.BlockSpec(memory_space=VMEM)


def sspec():
    return pl.BlockSpec(memory_space=SMEM)


def cost(flops, nbytes):
    return pl.CostEstimate(flops=flops, transcendentals=0, bytes_accessed=nbytes)


def select_kernel(index, place, routes, weights, tokens, *outs):
    rows_out, (sel_out, selw_out) = outs[: len(CHUNKS)], outs[len(CHUNKS) :]
    me = index[0].astype(f32)
    a = lax.broadcasted_iota(jnp.int32, (SLOTS, SLOTS), 0)
    b = lax.broadcasted_iota(jnp.int32, (SLOTS, SLOTS), 1)
    row = place[...].astype(f32)
    col = jnp.sum(jnp.where(a == b, row, 0.0), axis=1, keepdims=True)
    same = jnp.where(jnp.abs(col - row) < 0.5, 1.0, 0.0)
    copies = jnp.sum(same, axis=1, keepdims=True)
    rank = jnp.sum(jnp.where(b < a, same, 0.0), axis=1, keepdims=True)
    turn = me - copies * jnp.floor((me + 0.5) / copies)
    active = jnp.abs(rank - turn) < 0.5
    hit = jnp.zeros((SLOTS, TOK), f32)
    wt = jnp.zeros((SLOTS, TOK), f32)
    for k in range(routes.shape[0]):
        match = (jnp.abs(routes[k : k + 1, :].astype(f32) - col) < 0.5) & active
        hit = hit + jnp.where(match, 1.0, 0.0)
        wt = wt + jnp.where(match, weights[k : k + 1, :], 0.0)
    t0 = lax.broadcasted_iota(jnp.int32, (TOK, TOK), 0)
    t1 = lax.broadcasted_iota(jnp.int32, (TOK, TOK), 1)
    before = jnp.where(t0 < t1, 1.0, 0.0).astype(bf16)
    pos = jnp.dot(hit.astype(bf16), before, preferred_element_type=f32)
    pos = jnp.where(hit > 0.5, pos, -1.0)
    want = lax.broadcasted_iota(jnp.int32, (CAP, TOK), 0).astype(f32)
    for j in range(SLOTS):
        chosen = jnp.abs(pos[j : j + 1, :] - want) < 0.5
        sel_out[j * CAP : (j + 1) * CAP, :] = jnp.where(chosen, 1.0, 0.0).astype(bf16)
        selw_out[j * CAP : (j + 1) * CAP, :] = jnp.where(chosen, wt[j : j + 1, :], 0.0)
    group = 8
    for j in range(0, SLOTS, group):
        sel = sel_out[j * CAP : (j + group) * CAP, :]
        got = jnp.dot(sel, tokens[...], preferred_element_type=f32).astype(bf16)
        got = got.reshape(group, CAP, QD)
        for (lo, hi), out in zip(CHUNKS, rows_out):
            out[j : j + group] = got[:, lo:hi]


def select_rows(index, placement, routes, weights, tokens):
    return pl.pallas_call(
        select_kernel,
        out_shape=[jax.ShapeDtypeStruct((SLOTS, hi - lo, QD), bf16) for lo, hi in CHUNKS]
        + [jax.ShapeDtypeStruct((ROWS, TOK), bf16), jax.ShapeDtypeStruct((ROWS, TOK), f32)],
        in_specs=[sspec()] + [vspec()] * 4,
        out_specs=[vspec()] * (len(CHUNKS) + 2),
        cost_estimate=cost(2 * ROWS * TOK * QD, 4 << 20),
        name="select_rows",
    )(index, placement[None, :], routes.T, weights.T, tokens)


def scale_kernel(sel, selw, cot, out):
    for r in range(0, SLOTS * CAP, 512):
        w = jnp.sum(selw[r : r + 512, :], axis=1, keepdims=True)
        picked = jnp.dot(sel[r : r + 512, :], cot[...], preferred_element_type=f32)
        out[r : r + 512, :] = (w * picked).astype(bf16)


def scale_rows(sel, selw, cot):
    rows = SLOTS * CAP
    return pl.pallas_call(
        scale_kernel,
        out_shape=jax.ShapeDtypeStruct((rows, QD), bf16),
        in_specs=[vspec()] * 3,
        out_specs=vspec(),
        cost_estimate=cost(2 * rows * TOK * QD, 4 << 20),
        name="scale_rows",
    )(sel, selw, cot)


def row_block(block, width):
    return pl.BlockSpec((block, width), lambda i: (i, 0))


def piece_specs(n, pieces):
    half = HALF // n
    specs = []
    for group in pieces:
        shape = (n,) + group[0].shape[1:]
        own = pl.BlockSpec(shape, lambda i: (i, 0, 0))
        low = pl.BlockSpec(shape, lambda i: (jnp.minimum(i, half - 1), 0, 0))
        high = pl.BlockSpec(shape, lambda i: (jnp.maximum(i - half, 0), 0, 0))
        specs += [own] + [low, high] * 3
    return specs


def whole(shape):
    return pl.BlockSpec(shape, lambda i: (0,) * len(shape))


def gather_pieces(n, dp, pieces, out):
    first = pl.program_id(0) < HALF // n
    at = 0
    for j in range(0, len(pieces), 7):
        own, la, lb, ra, rb, fa, fb = pieces[j : j + 7]
        rows, width = own.shape[1:]
        for shift, x in (
            (0, own[...]),
            (3, jnp.where(first, la[...], lb[...])),
            (1, jnp.where(first, ra[...], rb[...])),
            (2, jnp.where(first, fa[...], fb[...])),
        ):
            q = lax.rem(dp[0] + shift, N_DP)
            out[:, at : at + rows, pl.ds(pl.multiple_of(q * width, width), width)] = x
        at += rows


def flat(pieces):
    return [x for group in pieces for x in group]


HIDDEN_SOURCES = 8


def hidden_kernel(count, dp, *refs):
    pieces, (wg, wu, g_out, u_out, h_out, gathered) = refs[:count], refs[count:]
    gather_pieces(HIDDEN_SOURCES, dp, pieces, gathered)
    x = gathered[...].reshape(HIDDEN_SOURCES * CAP, D)
    g = jnp.dot(x, wg[...], preferred_element_type=f32) * scale_in
    u = jnp.dot(x, wu[...], preferred_element_type=f32) * scale_in
    g_out[...] = g
    u_out[...] = u
    h_out[...] = (g / (1.0 + jnp.exp(-g)) * u).astype(bf16)


def hidden_of(dp, pieces, wg, wu):
    n = HIDDEN_SOURCES
    block = n * CAP
    inputs = flat(pieces)
    return pl.pallas_call(
        functools.partial(hidden_kernel, len(inputs)),
        grid=(SLOTS // n,),
        out_shape=[
            jax.ShapeDtypeStruct((ROWS, QF), f32),
            jax.ShapeDtypeStruct((ROWS, QF), f32),
            jax.ShapeDtypeStruct((ROWS, QF), bf16),
        ],
        in_specs=[sspec()] + piece_specs(n, pieces) + [whole((D, QF)), whole((D, QF))],
        out_specs=[row_block(block, QF)] * 3,
        scratch_shapes=[VMEM((n, CAP, D), bf16)],
        cost_estimate=cost(4 * ROWS * D * QF, ROWS * D * 2 + 8 * D * QF),
        name="hidden",
    )(dp, *inputs, wg, wu)


PARTIAL_BLOCK = 384


def partial_kernel(dp, x, wd, *outs):
    for k, out in enumerate(outs):
        q = lax.rem(dp[0] + k, N_DP)
        out[...] = lax.dot_general(
            x[...],
            wd[pl.ds(pl.multiple_of(q * QF, QF), QF), :],
            (((1,), (1,)), ((), ())),
            preferred_element_type=f32,
        ).astype(bf16)


def partial_grads(dp, x, wd):
    block = PARTIAL_BLOCK
    return pl.pallas_call(
        partial_kernel,
        grid=(ROWS // block,),
        out_shape=[jax.ShapeDtypeStruct((ROWS, QF), bf16)] * N_DP,
        in_specs=[sspec(), row_block(block, QD), whole((FF, QD))],
        out_specs=[row_block(block, QF)] * N_DP,
        cost_estimate=cost(2 * ROWS * QD * FF, 6 << 20),
        name="partial_grads",
    )(dp, x, wd)


WEIGHT_SOURCES = 16


def weight_kernel(count, dp, h0, h1, h2, h3, g_in, u_in, *refs):
    pieces, (out, gathered, acc) = refs[:count], refs[count:]
    i = pl.program_id(0)
    gather_pieces(WEIGHT_SOURCES, dp, pieces, gathered)
    x = gathered[...].reshape(WEIGHT_SOURCES * CAP, D)
    grad = h0[...].astype(f32) + h1[...].astype(f32) + h2[...].astype(f32) + h3[...].astype(f32)
    grad = grad * scale_mid
    g = g_in[...]
    s = 1.0 / (1.0 + jnp.exp(-g))
    gg = (grad * u_in[...] * s * (1.0 + g * (1.0 - s))).astype(bf16)
    part = lax.dot_general(gg, x, (((0,), (0,)), ((), ())), preferred_element_type=f32)

    @pl.when(i == 0)
    def _():
        acc[...] = part

    @pl.when(i == pl.num_programs(0) - 1)
    def _():
        for r in range(0, D, 512):
            total = (acc[:, r : r + 512] + part[:, r : r + 512]) * scale_in
            out[r : r + 512, :] = total.T.astype(bf16)


def weight_grads(dp, hg, g, u, pieces):
    n = WEIGHT_SOURCES
    block = n * CAP
    inputs = flat(pieces)
    assert SLOTS // n == 2
    return pl.pallas_call(
        functools.partial(weight_kernel, len(inputs)),
        grid=(SLOTS // n,),
        out_shape=jax.ShapeDtypeStruct((D, QF), bf16),
        in_specs=[sspec()] + [row_block(block, QF)] * 6 + piece_specs(n, pieces),
        out_specs=whole((D, QF)),
        scratch_shapes=[VMEM((n, CAP, D), bf16), VMEM((QF, D), f32)],
        cost_estimate=cost(2 * ROWS * D * QF, ROWS * D * 2 + (8 << 20)),
        name="weight_grads",
    )(dp, *hg, g, u, *inputs)


OUTPUT_SOURCES = 8


def output_kernel(count, dp, *refs):
    pieces, (wd, out, gathered) = refs[:count], refs[count:]
    gather_pieces(OUTPUT_SOURCES, dp, pieces, gathered)
    x = gathered[...].reshape(OUTPUT_SOURCES * CAP, FF)
    total = jnp.dot(x, wd[...], preferred_element_type=f32)
    out[...] = (total * scale_mid).astype(bf16)


def outputs_of(dp, pieces, wd):
    n = OUTPUT_SOURCES
    inputs = flat(pieces)
    return pl.pallas_call(
        functools.partial(output_kernel, len(inputs)),
        grid=(SLOTS // n,),
        out_shape=jax.ShapeDtypeStruct((ROWS, QD), bf16),
        in_specs=[sspec()] + piece_specs(n, pieces) + [whole((FF, QD))],
        out_specs=row_block(n * CAP, QD),
        scratch_shapes=[VMEM((n, CAP, FF), bf16)],
        cost_estimate=cost(2 * ROWS * FF * QD, ROWS * (FF + QD) * 2),
        name="outputs",
    )(dp, *inputs, wd)


def combine_kernel(selw, *refs):
    out = refs[-1]
    total = jnp.zeros(out.shape, f32)
    base = 0
    for ref in refs[:-1]:
        n = ref.shape[0]
        w = selw[base : base + n, :]
        high = w.astype(bf16)
        low = (w - high.astype(f32)).astype(bf16)
        rows = ref[...]
        for part in (high, low):
            total = total + lax.dot_general(
                part, rows, (((0,), (0,)), ((), ())), preferred_element_type=f32
            )
        base += n
    out[...] = total.astype(bf16)


def combine(selw, rows):
    return pl.pallas_call(
        combine_kernel,
        out_shape=jax.ShapeDtypeStruct((TOK, QD), bf16),
        in_specs=[vspec()] * (1 + len(rows)),
        out_specs=vspec(),
        cost_estimate=cost(4 * SLOTS * CAP * TOK * QD, 4 << 20),
        name="combine",
    )(selw, *rows)


UPDATE_ROWS = 16


def update_kernel(plan, placement, grads, gate, first, second, out, total):
    total[...] = jnp.zeros_like(total)
    for s in range(SLOTS):
        total[placement[s]] += grads[s].astype(f32)

    def body(s, carry):
        p = plan[s]
        g = total[placement[p]]
        one = beta_first * first[p].astype(f32) + (1.0 - beta_first) * g
        two = beta_second * second[p].astype(f32) + (1.0 - beta_second) * g * g
        kept = gate[p].astype(f32) * (1.0 - learn_rate * weight_decay)
        out[s, 0] = (kept - learn_rate * one / (jnp.sqrt(two) + epsilon)).astype(bf16)
        out[s, 1] = one.astype(bf16)
        out[s, 2] = two.astype(bf16)
        return carry

    lax.fori_loop(0, SLOTS, body, 0, unroll=4)


def update(plan, placement, grads, states):
    steps = PART // UPDATE_ROWS

    def part(n):
        return pl.BlockSpec((SLOTS, UPDATE_ROWS, QF), lambda i, *_: (0, n * steps + i, 0))

    return pl.pallas_call(
        update_kernel,
        grid_spec=pltpu.PrefetchScalarGridSpec(
            num_scalar_prefetch=2,
            grid=(steps,),
            in_specs=[part(0), part(0), part(1), part(2)],
            out_specs=pl.BlockSpec((SLOTS, 3, UPDATE_ROWS, QF), lambda i, *_: (0, 0, i, 0)),
            scratch_shapes=[VMEM((SLOTS, UPDATE_ROWS, QF), f32)],
        ),
        out_shape=jax.ShapeDtypeStruct((SLOTS, 3, PART, QF), bf16),
        cost_estimate=cost(20 * D * SLOTS * QF // SLOTS, 10 << 20),
        name="update",
    )(plan, placement, grads, states, states, states)


def finish_kernel(moments, *outs):
    for k, out in enumerate(outs):
        out[...] = moments[:, k]


def finish(moments):
    n = 8
    part = pl.BlockSpec((n, PART, QF), lambda i: (i, 0, 0))
    return pl.pallas_call(
        finish_kernel,
        grid=(SLOTS // n,),
        out_shape=[jax.ShapeDtypeStruct((SLOTS, PART, QF), bf16)] * 3,
        in_specs=[pl.BlockSpec((n, 3, PART, QF), lambda i: (i, 0, 0, 0))],
        out_specs=[part] * 3,
        cost_estimate=cost(0, 12 << 20),
        name="finish",
    )(moments)


def exchange(x):
    return lax.all_to_all(x, "expert", split_axis=0, concat_axis=0, tiled=True)


def shift(x, by):
    return lax.ppermute(x, "dp", [(i, (i + by) % N_DP) for i in range(N_DP)])


def ring(x):
    low, high = x[:HALF], x[HALF:]
    la = shift(low, 1)
    rb = shift(high, -1)
    lb = shift(high, 1)
    ra = shift(low, -1)
    fa = shift(la, 1)
    fb = shift(rb, -1)
    return (x, la, lb, ra, rb, fa, fb)


def device_step(
    tokens,
    cotangent,
    routes,
    route_weight,
    gate_weight,
    up_weight,
    down_weight,
    first_moment,
    second_moment,
    placement,
    migration_plan,
):
    index = lax.axis_index("expert").astype(jnp.int32)[None]
    dp = lax.axis_index("dp").astype(jnp.int32)[None]
    wg, wu, wd = gate_weight[0], up_weight[0], down_weight[0]
    *rows, sel, selw = select_rows(index, placement, routes, route_weight, tokens)
    got = [exchange(x) for x in rows]
    sent_grads = scale_rows(sel, selw, cotangent)
    got_grads = exchange(sent_grads.reshape(SLOTS, CAP, QD)).reshape(ROWS, QD)
    packed = jnp.concatenate(
        [x[0].reshape(SLOTS, PART, QF) for x in (gate_weight, first_moment, second_moment)],
        axis=1,
    )
    states = exchange(packed)
    pieces = [ring(x) for x in got]
    g, u, h = hidden_of(dp, pieces, wg, wu)
    partials = partial_grads(dp, got_grads, wd)
    hg = [partials[0]] + [shift(partials[k], k) for k in range(1, N_DP)]
    wgrad = weight_grads(dp, hg, g, u, pieces)
    got_wgrad = exchange(wgrad.reshape(SLOTS, PART, QF))
    moments = exchange(update(migration_plan, placement, got_wgrad, states))
    out = outputs_of(dp, [ring(h.reshape(SLOTS, CAP, QF))], wd)
    returned = exchange(out.reshape(SLOTS, CAP, QD)).reshape(ROWS, QD)
    layer_output = combine(selw, [returned])
    results = finish(moments)
    return (layer_output,) + tuple(r.reshape(1, D, QF) for r in results)


def solution(mesh):
    placed = (
        P("expert", "dp"),
        P("expert", "dp"),
        P("expert", None),
        P("expert", None),
        P("expert", None, "dp"),
        P("expert", None, "dp"),
        P("expert", None, "dp"),
        P("expert", None, "dp"),
        P("expert", None, "dp"),
        P(),
        P(),
    )
    return jax.shard_map(
        device_step,
        mesh=mesh,
        in_specs=placed,
        out_specs=(
            P("expert", "dp"),
            P("expert", None, "dp"),
            P("expert", None, "dp"),
            P("expert", None, "dp"),
        ),
        check_vma=False,
    )
```

```python
import functools
import math

import jax
import jax.numpy as jnp
from jax import lax
from jax.experimental import pallas as pl
from jax.experimental.pallas import tpu as pltpu
from jax.sharding import PartitionSpec as P


D = 3584
FF = 1024
N_DP = 4
SLOTS = 32
CAP = 48
TOK = 128
QD = D // N_DP
QF = FF // N_DP
PART = D // SLOTS
CHUNKS = ((0, 16), (16, 48))
ROWS = SLOTS * CAP
HALF = SLOTS // 2

beta_first = 0.9
beta_second = 0.95
learn_rate = 0.02
weight_decay = 0.1
epsilon = 1e-08
scale_in = 1.0 / math.sqrt(D)
scale_mid = 1.0 / math.sqrt(FF)


f32 = jnp.float32
bf16 = jnp.bfloat16
VMEM = pltpu.VMEM
SMEM = pltpu.SMEM


def vspec():
    return pl.BlockSpec(memory_space=VMEM)


def sspec():
    return pl.BlockSpec(memory_space=SMEM)


def cost(flops, nbytes):
    return pl.CostEstimate(flops=flops, transcendentals=0, bytes_accessed=nbytes)


def select_kernel(index, place, routes, weights, tokens, *outs):
    rows_out, (sel_out, selw_out) = outs[: len(CHUNKS)], outs[len(CHUNKS) :]
    me = index[0].astype(f32)
    a = lax.broadcasted_iota(jnp.int32, (SLOTS, SLOTS), 0)
    b = lax.broadcasted_iota(jnp.int32, (SLOTS, SLOTS), 1)
    row = place[...].astype(f32)
    col = jnp.sum(jnp.where(a == b, row, 0.0), axis=1, keepdims=True)
    same = jnp.where(jnp.abs(col - row) < 0.5, 1.0, 0.0)
    copies = jnp.sum(same, axis=1, keepdims=True)
    rank = jnp.sum(jnp.where(b < a, same, 0.0), axis=1, keepdims=True)
    turn = me - copies * jnp.floor((me + 0.5) / copies)
    active = jnp.abs(rank - turn) < 0.5
    hit = jnp.zeros((SLOTS, TOK), f32)
    wt = jnp.zeros((SLOTS, TOK), f32)
    for k in range(routes.shape[0]):
        match = (jnp.abs(routes[k : k + 1, :].astype(f32) - col) < 0.5) & active
        hit = hit + jnp.where(match, 1.0, 0.0)
        wt = wt + jnp.where(match, weights[k : k + 1, :], 0.0)
    t0 = lax.broadcasted_iota(jnp.int32, (TOK, TOK), 0)
    t1 = lax.broadcasted_iota(jnp.int32, (TOK, TOK), 1)
    before = jnp.where(t0 < t1, 1.0, 0.0).astype(bf16)
    pos = jnp.dot(hit.astype(bf16), before, preferred_element_type=f32)
    pos = jnp.where(hit > 0.5, pos, -1.0)
    want = lax.broadcasted_iota(jnp.int32, (CAP, TOK), 0).astype(f32)
    for j in range(SLOTS):
        chosen = jnp.abs(pos[j : j + 1, :] - want) < 0.5
        sel_out[j * CAP : (j + 1) * CAP, :] = jnp.where(chosen, 1.0, 0.0).astype(bf16)
        selw_out[j * CAP : (j + 1) * CAP, :] = jnp.where(chosen, wt[j : j + 1, :], 0.0)
    group = 8
    for j in range(0, SLOTS, group):
        sel = sel_out[j * CAP : (j + group) * CAP, :]
        got = jnp.dot(sel, tokens[...], preferred_element_type=f32).astype(bf16)
        got = got.reshape(group, CAP, QD)
        for (lo, hi), out in zip(CHUNKS, rows_out):
            out[j : j + group] = got[:, lo:hi]


def select_rows(index, placement, routes, weights, tokens):
    return pl.pallas_call(
        select_kernel,
        out_shape=[jax.ShapeDtypeStruct((SLOTS, hi - lo, QD), bf16) for lo, hi in CHUNKS]
        + [jax.ShapeDtypeStruct((ROWS, TOK), bf16), jax.ShapeDtypeStruct((ROWS, TOK), f32)],
        in_specs=[sspec()] + [vspec()] * 4,
        out_specs=[vspec()] * (len(CHUNKS) + 2),
        cost_estimate=cost(2 * ROWS * TOK * QD, 4 << 20),
        name="select_rows",
    )(index, placement[None, :], routes.T, weights.T, tokens)


def scale_kernel(sel, selw, cot, out):
    for r in range(0, SLOTS * CAP, 512):
        w = jnp.sum(selw[r : r + 512, :], axis=1, keepdims=True)
        picked = jnp.dot(sel[r : r + 512, :], cot[...], preferred_element_type=f32)
        out[r : r + 512, :] = (w * picked).astype(bf16)


def scale_rows(sel, selw, cot):
    rows = SLOTS * CAP
    return pl.pallas_call(
        scale_kernel,
        out_shape=jax.ShapeDtypeStruct((rows, QD), bf16),
        in_specs=[vspec()] * 3,
        out_specs=vspec(),
        cost_estimate=cost(2 * rows * TOK * QD, 4 << 20),
        name="scale_rows",
    )(sel, selw, cot)


def row_block(block, width):
    return pl.BlockSpec((block, width), lambda i: (i, 0))


def piece_specs(n, pieces):
    half = HALF // n
    specs = []
    for group in pieces:
        shape = (n,) + group[0].shape[1:]
        own = pl.BlockSpec(shape, lambda i: (i, 0, 0))
        low = pl.BlockSpec(shape, lambda i: (jnp.minimum(i, half - 1), 0, 0))
        high = pl.BlockSpec(shape, lambda i: (jnp.maximum(i - half, 0), 0, 0))
        specs += [own] + [low, high] * 3
    return specs


def whole(shape):
    return pl.BlockSpec(shape, lambda i: (0,) * len(shape))


def gather_pieces(n, dp, pieces, out):
    first = pl.program_id(0) < HALF // n
    at = 0
    for j in range(0, len(pieces), 7):
        own, la, lb, ra, rb, fa, fb = pieces[j : j + 7]
        rows, width = own.shape[1:]
        for shift, x in (
            (0, own[...]),
            (3, jnp.where(first, la[...], lb[...])),
            (1, jnp.where(first, ra[...], rb[...])),
            (2, jnp.where(first, fa[...], fb[...])),
        ):
            q = lax.rem(dp[0] + shift, N_DP)
            out[:, at : at + rows, pl.ds(pl.multiple_of(q * width, width), width)] = x
        at += rows


def flat(pieces):
    return [x for group in pieces for x in group]


HIDDEN_SOURCES = 8


def hidden_kernel(count, dp, *refs):
    pieces, (wg, wu, g_out, u_out, h_out, gathered) = refs[:count], refs[count:]
    gather_pieces(HIDDEN_SOURCES, dp, pieces, gathered)
    x = gathered[...].reshape(HIDDEN_SOURCES * CAP, D)
    g = jnp.dot(x, wg[...], preferred_element_type=f32) * scale_in
    u = jnp.dot(x, wu[...], preferred_element_type=f32) * scale_in
    g_out[...] = g
    u_out[...] = u
    h_out[...] = (g / (1.0 + jnp.exp(-g)) * u).astype(bf16)


def hidden_of(dp, pieces, wg, wu):
    n = HIDDEN_SOURCES
    block = n * CAP
    inputs = flat(pieces)
    return pl.pallas_call(
        functools.partial(hidden_kernel, len(inputs)),
        grid=(SLOTS // n,),
        out_shape=[
            jax.ShapeDtypeStruct((ROWS, QF), f32),
            jax.ShapeDtypeStruct((ROWS, QF), f32),
            jax.ShapeDtypeStruct((ROWS, QF), bf16),
        ],
        in_specs=[sspec()] + piece_specs(n, pieces) + [whole((D, QF)), whole((D, QF))],
        out_specs=[row_block(block, QF)] * 3,
        scratch_shapes=[VMEM((n, CAP, D), bf16)],
        cost_estimate=cost(4 * ROWS * D * QF, ROWS * D * 2 + 8 * D * QF),
        name="hidden",
    )(dp, *inputs, wg, wu)


PARTIAL_BLOCK = 384


def partial_kernel(dp, x, wd, *outs):
    for k, out in enumerate(outs):
        q = lax.rem(dp[0] + k, N_DP)
        out[...] = lax.dot_general(
            x[...],
            wd[pl.ds(pl.multiple_of(q * QF, QF), QF), :],
            (((1,), (1,)), ((), ())),
            preferred_element_type=f32,
        ).astype(bf16)


def partial_grads(dp, x, wd, part):
    block = PARTIAL_BLOCK
    rows = ROWS // 2
    steps = rows // block
    return pl.pallas_call(
        partial_kernel,
        grid=(steps,),
        out_shape=[jax.ShapeDtypeStruct((rows, QF), bf16)] * N_DP,
        in_specs=[
            sspec(),
            pl.BlockSpec((block, QD), lambda i: (part * steps + i, 0)),
            whole((FF, QD)),
        ],
        out_specs=[row_block(block, QF)] * N_DP,
        cost_estimate=cost(2 * rows * QD * FF, 4 << 20),
    )(dp, x, wd)


WEIGHT_SOURCES = 8
WEIGHT_STEPS = HALF // WEIGHT_SOURCES


def weight_kernel(part, count, dp, h0, h1, h2, h3, g_in, u_in, *refs):
    pieces, rest = refs[:count], refs[count:]
    i = pl.program_id(0)
    out, gathered, acc = rest[-3:]
    at = 0
    for j in range(0, count, 4):
        rows = pieces[j].shape[1]
        for shift, ref in zip((0, 3, 1, 2), pieces[j : j + 4]):
            q = lax.rem(dp[0] + shift, N_DP)
            gathered[:, at : at + rows, pl.ds(pl.multiple_of(q * QD, QD), QD)] = ref[...]
        at += rows
    x = gathered[...].reshape(WEIGHT_SOURCES * CAP, D)
    grad = h0[...].astype(f32) + h1[...].astype(f32) + h2[...].astype(f32) + h3[...].astype(f32)
    grad = grad * scale_mid
    g = g_in[...]
    s = 1.0 / (1.0 + jnp.exp(-g))
    gg = (grad * u_in[...] * s * (1.0 + g * (1.0 - s))).astype(bf16)
    product = lax.dot_general(gg, x, (((0,), (0,)), ((), ())), preferred_element_type=f32)
    last = i == pl.num_programs(0) - 1
    if part == 0:

        @pl.when(i == 0)
        def _():
            out[...] = product

        @pl.when(i > 0)
        def _():
            out[...] += product

    else:

        @pl.when(i == 0)
        def _():
            acc[...] = rest[0][...] + product

        @pl.when(last)
        def _():
            for r in range(0, D, 512):
                total = (acc[:, r : r + 512] + product[:, r : r + 512]) * scale_in
                out[r : r + 512, :] = total.T.astype(bf16)


def weight_grads(dp, hg, g, u, pieces, part, carry=()):
    n = WEIGHT_SOURCES
    block = n * CAP
    steps = WEIGHT_STEPS
    assert steps == 2
    inputs, specs = [], []
    for own, la, lb, ra, rb, fa, fb in pieces:
        shape = (n,) + own.shape[1:]
        inputs += [own] + ([la, ra, fa] if part == 0 else [lb, rb, fb])
        specs += [pl.BlockSpec(shape, lambda i: (part * steps + i, 0, 0))]
        specs += [pl.BlockSpec(shape, lambda i: (i, 0, 0))] * 3
    values = pl.BlockSpec((block, QF), lambda i: (part * steps + i, 0))
    shape = jax.ShapeDtypeStruct((QF, D), f32) if part == 0 else jax.ShapeDtypeStruct((D, QF), bf16)
    return pl.pallas_call(
        functools.partial(weight_kernel, part, len(inputs)),
        grid=(steps,),
        out_shape=shape,
        in_specs=[sspec()]
        + [row_block(block, QF)] * 4
        + [values] * 2
        + specs
        + [whole((QF, D))] * len(carry),
        out_specs=whole(shape.shape),
        scratch_shapes=[VMEM((n, CAP, D), bf16), VMEM((QF, D) if part else (8, 128), f32)],
        cost_estimate=cost(ROWS * D * QF, ROWS * D + (8 << 20)),
    )(dp, *hg, g, u, *inputs, *carry)


OUTPUT_SOURCES = 8


def output_kernel(count, dp, *refs):
    pieces, (wd, out, gathered) = refs[:count], refs[count:]
    gather_pieces(OUTPUT_SOURCES, dp, pieces, gathered)
    x = gathered[...].reshape(OUTPUT_SOURCES * CAP, FF)
    total = jnp.dot(x, wd[...], preferred_element_type=f32)
    out[...] = (total * scale_mid).astype(bf16)


def outputs_of(dp, pieces, wd):
    n = OUTPUT_SOURCES
    inputs = flat(pieces)
    return pl.pallas_call(
        functools.partial(output_kernel, len(inputs)),
        grid=(SLOTS // n,),
        out_shape=jax.ShapeDtypeStruct((ROWS, QD), bf16),
        in_specs=[sspec()] + piece_specs(n, pieces) + [whole((FF, QD))],
        out_specs=row_block(n * CAP, QD),
        scratch_shapes=[VMEM((n, CAP, FF), bf16)],
        cost_estimate=cost(2 * ROWS * FF * QD, ROWS * (FF + QD) * 2),
        name="outputs",
    )(dp, *inputs, wd)


def combine_kernel(selw, *refs):
    out = refs[-1]
    total = jnp.zeros(out.shape, f32)
    base = 0
    for ref in refs[:-1]:
        n = ref.shape[0]
        w = selw[base : base + n, :]
        high = w.astype(bf16)
        low = (w - high.astype(f32)).astype(bf16)
        rows = ref[...]
        for part in (high, low):
            total = total + lax.dot_general(
                part, rows, (((0,), (0,)), ((), ())), preferred_element_type=f32
            )
        base += n
    out[...] = total.astype(bf16)


def combine(selw, rows):
    return pl.pallas_call(
        combine_kernel,
        out_shape=jax.ShapeDtypeStruct((TOK, QD), bf16),
        in_specs=[vspec()] * (1 + len(rows)),
        out_specs=vspec(),
        cost_estimate=cost(4 * SLOTS * CAP * TOK * QD, 4 << 20),
        name="combine",
    )(selw, *rows)


UPDATE_ROWS = 16


def update_kernel(plan, placement, grads, gate, first, second, out, total):
    total[...] = jnp.zeros_like(total)
    for s in range(SLOTS):
        total[placement[s]] += grads[s].astype(f32)

    def body(s, carry):
        p = plan[s]
        g = total[placement[p]]
        one = beta_first * first[p].astype(f32) + (1.0 - beta_first) * g
        two = beta_second * second[p].astype(f32) + (1.0 - beta_second) * g * g
        kept = gate[p].astype(f32) * (1.0 - learn_rate * weight_decay)
        out[s, 0] = (kept - learn_rate * one / (jnp.sqrt(two) + epsilon)).astype(bf16)
        out[s, 1] = one.astype(bf16)
        out[s, 2] = two.astype(bf16)
        return carry

    lax.fori_loop(0, SLOTS, body, 0, unroll=4)


def update(plan, placement, grads, states):
    steps = PART // UPDATE_ROWS

    def part(n):
        return pl.BlockSpec((SLOTS, UPDATE_ROWS, QF), lambda i, *_: (0, n * steps + i, 0))

    return pl.pallas_call(
        update_kernel,
        grid_spec=pltpu.PrefetchScalarGridSpec(
            num_scalar_prefetch=2,
            grid=(steps,),
            in_specs=[part(0), part(0), part(1), part(2)],
            out_specs=pl.BlockSpec((SLOTS, 3, UPDATE_ROWS, QF), lambda i, *_: (0, 0, i, 0)),
            scratch_shapes=[VMEM((SLOTS, UPDATE_ROWS, QF), f32)],
        ),
        out_shape=jax.ShapeDtypeStruct((SLOTS, 3, PART, QF), bf16),
        cost_estimate=cost(20 * D * SLOTS * QF // SLOTS, 10 << 20),
        name="update",
    )(plan, placement, grads, states, states, states)


def finish_kernel(moments, *outs):
    for k, out in enumerate(outs):
        out[...] = moments[:, k]


def finish(moments):
    n = 8
    part = pl.BlockSpec((n, PART, QF), lambda i: (i, 0, 0))
    return pl.pallas_call(
        finish_kernel,
        grid=(SLOTS // n,),
        out_shape=[jax.ShapeDtypeStruct((SLOTS, PART, QF), bf16)] * 3,
        in_specs=[pl.BlockSpec((n, 3, PART, QF), lambda i: (i, 0, 0, 0))],
        out_specs=[part] * 3,
        cost_estimate=cost(0, 12 << 20),
        name="finish",
    )(moments)


def exchange(x):
    return lax.all_to_all(x, "expert", split_axis=0, concat_axis=0, tiled=True)


def shift(x, by):
    return lax.ppermute(x, "dp", [(i, (i + by) % N_DP) for i in range(N_DP)])


def ring(x):
    low, high = x[:HALF], x[HALF:]
    la = shift(low, 1)
    rb = shift(high, -1)
    lb = shift(high, 1)
    ra = shift(low, -1)
    fa = shift(la, 1)
    fb = shift(rb, -1)
    return (x, la, lb, ra, rb, fa, fb)


def device_step(
    tokens,
    cotangent,
    routes,
    route_weight,
    gate_weight,
    up_weight,
    down_weight,
    first_moment,
    second_moment,
    placement,
    migration_plan,
):
    index = lax.axis_index("expert").astype(jnp.int32)[None]
    dp = lax.axis_index("dp").astype(jnp.int32)[None]
    wg, wu, wd = gate_weight[0], up_weight[0], down_weight[0]
    *rows, sel, selw = select_rows(index, placement, routes, route_weight, tokens)
    got = [exchange(x) for x in rows]
    sent_grads = scale_rows(sel, selw, cotangent)
    got_grads = exchange(sent_grads.reshape(SLOTS, CAP, QD)).reshape(ROWS, QD)
    packed = jnp.concatenate(
        [x[0].reshape(SLOTS, PART, QF) for x in (gate_weight, first_moment, second_moment)],
        axis=1,
    )
    states = exchange(packed)
    pieces = [ring(x) for x in got]
    g, u, h = hidden_of(dp, pieces, wg, wu)
    carry = ()
    hg = []
    for part in range(2):
        partials = partial_grads(dp, got_grads, wd, part)
        hg.append([partials[0]] + [shift(partials[k], k) for k in range(1, N_DP)])
    for part in range(2):
        carry = (weight_grads(dp, hg[part], g, u, pieces, part, carry),)
    wgrad = carry[0]
    got_wgrad = exchange(wgrad.reshape(SLOTS, PART, QF))
    moments = exchange(update(migration_plan, placement, got_wgrad, states))
    out = outputs_of(dp, [ring(h.reshape(SLOTS, CAP, QF))], wd)
    returned = exchange(out.reshape(SLOTS, CAP, QD)).reshape(ROWS, QD)
    layer_output = combine(selw, [returned])
    results = finish(moments)
    return (layer_output,) + tuple(r.reshape(1, D, QF) for r in results)


def solution(mesh):
    placed = (
        P("expert", "dp"),
        P("expert", "dp"),
        P("expert", None),
        P("expert", None),
        P("expert", None, "dp"),
        P("expert", None, "dp"),
        P("expert", None, "dp"),
        P("expert", None, "dp"),
        P("expert", None, "dp"),
        P(),
        P(),
    )
    return jax.shard_map(
        device_step,
        mesh=mesh,
        in_specs=placed,
        out_specs=(
            P("expert", "dp"),
            P("expert", None, "dp"),
            P("expert", None, "dp"),
            P("expert", None, "dp"),
        ),
        check_vma=False,
    )
```

```python
import functools
import math

import jax
import jax.numpy as jnp
from jax import lax
from jax.experimental import pallas as pl
from jax.experimental.pallas import tpu as pltpu
from jax.sharding import PartitionSpec as P


D = 3584
FF = 1024
N_DP = 4
SLOTS = 32
CAP = 48
TOK = 128
QD = D // N_DP
QF = FF // N_DP
PART = D // SLOTS
CHUNKS = ((0, 16), (16, 48))
ROWS = SLOTS * CAP
HALF = SLOTS // 2

beta_first = 0.9
beta_second = 0.95
learn_rate = 0.02
weight_decay = 0.1
epsilon = 1e-08
scale_in = 1.0 / math.sqrt(D)
scale_mid = 1.0 / math.sqrt(FF)


f32 = jnp.float32
bf16 = jnp.bfloat16
VMEM = pltpu.VMEM
SMEM = pltpu.SMEM


def vspec():
    return pl.BlockSpec(memory_space=VMEM)


def sspec():
    return pl.BlockSpec(memory_space=SMEM)


def cost(flops, nbytes):
    return pl.CostEstimate(flops=flops, transcendentals=0, bytes_accessed=nbytes)


def select_kernel(index, place, routes, weights, tokens, out, pos_out, wt_out, sel):
    me = index[0].astype(f32)
    a = lax.broadcasted_iota(jnp.int32, (SLOTS, SLOTS), 0)
    b = lax.broadcasted_iota(jnp.int32, (SLOTS, SLOTS), 1)
    row = place[...].astype(f32)
    col = jnp.sum(jnp.where(a == b, row, 0.0), axis=1, keepdims=True)
    same = jnp.where(jnp.abs(col - row) < 0.5, 1.0, 0.0)
    copies = jnp.sum(same, axis=1, keepdims=True)
    rank = jnp.sum(jnp.where(b < a, same, 0.0), axis=1, keepdims=True)
    turn = me - copies * jnp.floor((me + 0.5) / copies)
    active = jnp.abs(rank - turn) < 0.5
    hit = jnp.zeros((SLOTS, TOK), f32)
    wt = jnp.zeros((SLOTS, TOK), f32)
    for k in range(routes.shape[0]):
        match = (jnp.abs(routes[k : k + 1, :].astype(f32) - col) < 0.5) & active
        hit = hit + jnp.where(match, 1.0, 0.0)
        wt = wt + jnp.where(match, weights[k : k + 1, :], 0.0)
    t0 = lax.broadcasted_iota(jnp.int32, (TOK, TOK), 0)
    t1 = lax.broadcasted_iota(jnp.int32, (TOK, TOK), 1)
    before = jnp.where(t0 < t1, 1.0, 0.0).astype(bf16)
    pos = jnp.dot(hit.astype(bf16), before, preferred_element_type=f32)
    pos = jnp.where(hit > 0.5, pos, -1.0)
    pos_out[...] = pos
    wt_out[...] = wt
    mark_rows(pos, wt, CHUNKS[0], sel, None)
    spread_rows(CHUNKS[0], sel, tokens, out)


def mark_rows(pos, wt, chunk, sel, selw):
    lo, hi = chunk
    want = (lax.broadcasted_iota(jnp.int32, (hi - lo, TOK), 0) + lo).astype(f32)
    for j in range(SLOTS):
        chosen = jnp.abs(pos[j : j + 1, :] - want) < 0.5
        if sel is not None:
            sel[j] = jnp.where(chosen, 1.0, 0.0).astype(bf16)
        if selw is not None:
            selw[j] = jnp.where(chosen, wt[j : j + 1, :], 0.0)


def spread_rows(chunk, sel, values, out):
    rows = chunk[1] - chunk[0]
    group = 256 // rows
    for j in range(0, SLOTS, group):
        picks = sel[j : j + group].reshape(group * rows, TOK)
        got = jnp.dot(picks, values[...], preferred_element_type=f32).astype(bf16)
        out[j : j + group] = got.reshape(group, rows, QD)


def select_rows(index, placement, routes, weights, tokens):
    rows = CHUNKS[0][1]
    return pl.pallas_call(
        select_kernel,
        out_shape=[
            jax.ShapeDtypeStruct((SLOTS, rows, QD), bf16),
            jax.ShapeDtypeStruct((SLOTS, TOK), f32),
            jax.ShapeDtypeStruct((SLOTS, TOK), f32),
        ],
        in_specs=[sspec()] + [vspec()] * 4,
        out_specs=[vspec()] * 3,
        scratch_shapes=[VMEM((SLOTS, rows, TOK), bf16)],
        cost_estimate=cost(2 * ROWS * TOK * QD // 3, 2 << 20),
        name="select_rows",
    )(index, placement[None, :], routes.T, weights.T, tokens)


def rest_kernel(pos_in, tokens, out, sel):
    pos = pos_in[...]
    mark_rows(pos, None, CHUNKS[1], sel, None)
    spread_rows(CHUNKS[1], sel, tokens, out)


def rest_rows(pos, tokens):
    lo, hi = CHUNKS[1]
    return pl.pallas_call(
        rest_kernel,
        out_shape=jax.ShapeDtypeStruct((SLOTS, hi - lo, QD), bf16),
        in_specs=[vspec()] * 2,
        out_specs=vspec(),
        scratch_shapes=[VMEM((SLOTS, hi - lo, TOK), bf16)],
        cost_estimate=cost(2 * ROWS * TOK * QD, 4 << 20),
        name="rest_rows",
    )(pos, tokens)


def scale_kernel(pos_in, wt_in, cot, out, high_out, low_out, selw):
    mark_rows(pos_in[...], wt_in[...], (0, CAP), None, selw)
    group = 8
    for j in range(0, SLOTS, group):
        w = selw[j : j + group].reshape(group * CAP, TOK)
        picks = jnp.where(w != 0.0, 1.0, 0.0).astype(bf16)
        picked = jnp.dot(picks, cot[...], preferred_element_type=f32)
        rows = pl.ds(j * CAP, group * CAP)
        out[rows, :] = (jnp.sum(w, axis=1, keepdims=True) * picked).astype(bf16)
        high = w.astype(bf16)
        high_out[rows, :] = high
        low_out[rows, :] = (w - high.astype(f32)).astype(bf16)


def scale_rows(pos, wt, cot):
    return pl.pallas_call(
        scale_kernel,
        out_shape=[
            jax.ShapeDtypeStruct((ROWS, QD), bf16),
            jax.ShapeDtypeStruct((ROWS, TOK), bf16),
            jax.ShapeDtypeStruct((ROWS, TOK), bf16),
        ],
        in_specs=[vspec()] * 3,
        out_specs=[vspec()] * 3,
        scratch_shapes=[VMEM((SLOTS, CAP, TOK), f32)],
        cost_estimate=cost(2 * ROWS * TOK * QD, 4 << 20),
        name="scale_rows",
    )(pos, wt, cot)


def row_block(block, width):
    return pl.BlockSpec((block, width), lambda i: (i, 0))


def piece_specs(n, pieces):
    half = HALF // n
    specs = []
    for group in pieces:
        shape = (n,) + group[0].shape[1:]
        own = pl.BlockSpec(shape, lambda i: (i, 0, 0))
        low = pl.BlockSpec(shape, lambda i: (jnp.minimum(i, half - 1), 0, 0))
        high = pl.BlockSpec(shape, lambda i: (jnp.maximum(i - half, 0), 0, 0))
        specs += [own] + [low, high] * 3
    return specs


def whole(shape):
    return pl.BlockSpec(shape, lambda i: (0,) * len(shape))


def gather_pieces(n, dp, pieces, out):
    first = pl.program_id(0) < HALF // n
    at = 0
    for j in range(0, len(pieces), 7):
        own, la, lb, ra, rb, fa, fb = pieces[j : j + 7]
        rows, width = own.shape[1:]
        for shift, x in (
            (0, own[...]),
            (3, jnp.where(first, la[...], lb[...])),
            (1, jnp.where(first, ra[...], rb[...])),
            (2, jnp.where(first, fa[...], fb[...])),
        ):
            q = lax.rem(dp[0] + shift, N_DP)
            out[:, at : at + rows, pl.ds(pl.multiple_of(q * width, width), width)] = x
        at += rows


def flat(pieces):
    return [x for group in pieces for x in group]


HIDDEN_SOURCES = 8


def hidden_kernel(count, dp, *refs):
    pieces, (wg, wu, slope_out, h_out, gathered) = refs[:count], refs[count:]
    gather_pieces(HIDDEN_SOURCES, dp, pieces, gathered)
    x = gathered[...].reshape(HIDDEN_SOURCES * CAP, D)
    g = jnp.dot(x, wg[...], preferred_element_type=f32) * scale_in
    u = jnp.dot(x, wu[...], preferred_element_type=f32) * scale_in
    s = 1.0 / (1.0 + jnp.exp(-g))
    slope_out[...] = u * s * (1.0 + g * (1.0 - s))
    h_out[...] = (g * s * u).astype(bf16)


def hidden_of(dp, pieces, wg, wu):
    n = HIDDEN_SOURCES
    block = n * CAP
    inputs = flat(pieces)
    return pl.pallas_call(
        functools.partial(hidden_kernel, len(inputs)),
        grid=(SLOTS // n,),
        out_shape=[
            jax.ShapeDtypeStruct((ROWS, QF), f32),
            jax.ShapeDtypeStruct((ROWS, QF), bf16),
        ],
        in_specs=[sspec()] + piece_specs(n, pieces) + [whole((D, QF)), whole((D, QF))],
        out_specs=[row_block(block, QF)] * 2,
        scratch_shapes=[VMEM((n, CAP, D), bf16)],
        cost_estimate=cost(4 * ROWS * D * QF, ROWS * D * 2 + 8 * D * QF),
        name="hidden",
    )(dp, *inputs, wg, wu)


PARTIAL_BLOCK = 384


def partial_kernel(dp, x, wd, *outs):
    for k, out in enumerate(outs):
        q = lax.rem(dp[0] + k, N_DP)
        out[...] = lax.dot_general(
            x[...],
            wd[pl.ds(pl.multiple_of(q * QF, QF), QF), :],
            (((1,), (1,)), ((), ())),
            preferred_element_type=f32,
        ).astype(bf16)


def partial_grads(dp, x, wd, part):
    block = PARTIAL_BLOCK
    rows = ROWS // 2
    steps = rows // block
    return pl.pallas_call(
        partial_kernel,
        grid=(steps,),
        out_shape=[jax.ShapeDtypeStruct((rows, QF), bf16)] * N_DP,
        in_specs=[
            sspec(),
            pl.BlockSpec((block, QD), lambda i: (part * steps + i, 0)),
            whole((FF, QD)),
        ],
        out_specs=[row_block(block, QF)] * N_DP,
        cost_estimate=cost(2 * rows * QD * FF, 4 << 20),
    )(dp, x, wd)


WEIGHT_SOURCES = 8
WEIGHT_STEPS = HALF // WEIGHT_SOURCES


def weight_kernel(part, count, dp, h0, h1, h2, h3, slope, *refs):
    pieces, rest = refs[:count], refs[count:]
    i = pl.program_id(0)
    out, acc = rest[-2:]
    grad = h0[...].astype(f32) + h1[...].astype(f32) + h2[...].astype(f32) + h3[...].astype(f32)
    gg = (grad * scale_mid * slope[...]).astype(bf16).reshape(WEIGHT_SOURCES, CAP, QF)
    at = 0
    groups = []
    for j in range(0, count, 4):
        rows = pieces[j].shape[1]
        groups.append(gg[:, at : at + rows].reshape(WEIGHT_SOURCES * rows, QF).T)
        at += rows
    for k, shift in enumerate((0, 3, 1, 2)):
        q = lax.rem(dp[0] + shift, N_DP)
        to = pl.ds(pl.multiple_of(q * QD, QD), QD)
        product = None
        for left, ref in zip(groups, pieces[k::4]):
            x = ref[...].reshape(-1, QD)
            one = jnp.dot(left, x, preferred_element_type=f32)
            product = one if product is None else product + one

        @pl.when(i == 0)
        def _():
            acc[:, to] = product if part == 0 else rest[0][:, to] + product

        @pl.when(i > 0)
        def _():
            if part == 0:
                out[:, to] = acc[:, to] + product
            else:
                total = ((acc[:, to] + product) * scale_in).astype(bf16)
                out[to, :] = total.T


def weight_grads(dp, hg, slope, pieces, part, carry=()):
    n = WEIGHT_SOURCES
    block = n * CAP
    steps = WEIGHT_STEPS
    assert steps == 2
    inputs, specs = [], []
    for own, la, lb, ra, rb, fa, fb in pieces:
        shape = (n,) + own.shape[1:]
        inputs += [own] + ([la, ra, fa] if part == 0 else [lb, rb, fb])
        specs += [pl.BlockSpec(shape, lambda i: (part * steps + i, 0, 0))]
        specs += [pl.BlockSpec(shape, lambda i: (i, 0, 0))] * 3
    values = pl.BlockSpec((block, QF), lambda i: (part * steps + i, 0))
    shape = jax.ShapeDtypeStruct((QF, D), f32) if part == 0 else jax.ShapeDtypeStruct((D, QF), bf16)
    return pl.pallas_call(
        functools.partial(weight_kernel, part, len(inputs)),
        grid=(steps,),
        out_shape=shape,
        in_specs=[sspec()]
        + [row_block(block, QF)] * 4
        + [values]
        + specs
        + [whole((QF, D))] * len(carry),
        out_specs=whole(shape.shape),
        scratch_shapes=[VMEM((QF, D), f32)],
        cost_estimate=cost(ROWS * D * QF, ROWS * D + (8 << 20)),
    )(dp, *hg, slope, *inputs, *carry)


OUTPUT_SOURCES = 8


def output_kernel(count, dp, *refs):
    pieces, (wd, out, gathered) = refs[:count], refs[count:]
    gather_pieces(OUTPUT_SOURCES, dp, pieces, gathered)
    x = gathered[...].reshape(OUTPUT_SOURCES * CAP, FF)
    total = jnp.dot(x, wd[...], preferred_element_type=f32)
    out[...] = (total * scale_mid).astype(bf16)


def outputs_of(dp, pieces, wd):
    n = OUTPUT_SOURCES
    inputs = flat(pieces)
    return pl.pallas_call(
        functools.partial(output_kernel, len(inputs)),
        grid=(SLOTS // n,),
        out_shape=jax.ShapeDtypeStruct((ROWS, QD), bf16),
        in_specs=[sspec()] + piece_specs(n, pieces) + [whole((FF, QD))],
        out_specs=row_block(n * CAP, QD),
        scratch_shapes=[VMEM((n, CAP, FF), bf16)],
        cost_estimate=cost(2 * ROWS * FF * QD, ROWS * (FF + QD) * 2),
        name="outputs",
    )(dp, *inputs, wd)


def combine_kernel(high, low, rows, out):
    total = jnp.zeros(out.shape, f32)
    for part in (high, low):
        total = total + lax.dot_general(
            part[...], rows[...], (((0,), (0,)), ((), ())), preferred_element_type=f32
        )
    out[...] = total.astype(bf16)


def combine(high, low, rows):
    return pl.pallas_call(
        combine_kernel,
        out_shape=jax.ShapeDtypeStruct((TOK, QD), bf16),
        in_specs=[vspec()] * 3,
        out_specs=vspec(),
        cost_estimate=cost(4 * ROWS * TOK * QD, 4 << 20),
        name="combine",
    )(high, low, rows)


UPDATE_ROWS = 16


def update_kernel(plan, placement, grads, gate, first, second, out, total):
    total[...] = jnp.zeros_like(total)
    for s in range(SLOTS):
        total[placement[s]] += grads[s].astype(f32)

    def body(s, carry):
        p = plan[s]
        g = total[placement[p]]
        one = beta_first * first[p].astype(f32) + (1.0 - beta_first) * g
        two = beta_second * second[p].astype(f32) + (1.0 - beta_second) * g * g
        kept = gate[p].astype(f32) * (1.0 - learn_rate * weight_decay)
        out[s, 0] = (kept - learn_rate * one / (jnp.sqrt(two) + epsilon)).astype(bf16)
        out[s, 1] = one.astype(bf16)
        out[s, 2] = two.astype(bf16)
        return carry

    lax.fori_loop(0, SLOTS, body, 0, unroll=4)


def update(plan, placement, grads, states):
    steps = PART // UPDATE_ROWS

    def part(n):
        return pl.BlockSpec((SLOTS, UPDATE_ROWS, QF), lambda i, *_: (0, n * steps + i, 0))

    return pl.pallas_call(
        update_kernel,
        grid_spec=pltpu.PrefetchScalarGridSpec(
            num_scalar_prefetch=2,
            grid=(steps,),
            in_specs=[part(0), part(0), part(1), part(2)],
            out_specs=pl.BlockSpec((SLOTS, 3, UPDATE_ROWS, QF), lambda i, *_: (0, 0, i, 0)),
            scratch_shapes=[VMEM((SLOTS, UPDATE_ROWS, QF), f32)],
        ),
        out_shape=jax.ShapeDtypeStruct((SLOTS, 3, PART, QF), bf16),
        cost_estimate=cost(20 * D * SLOTS * QF // SLOTS, 10 << 20),
        name="update",
    )(plan, placement, grads, states, states, states)


def finish_kernel(moments, *outs):
    for k, out in enumerate(outs):
        out[...] = moments[:, k]


def finish(moments):
    n = 8
    part = pl.BlockSpec((n, PART, QF), lambda i: (i, 0, 0))
    return pl.pallas_call(
        finish_kernel,
        grid=(SLOTS // n,),
        out_shape=[jax.ShapeDtypeStruct((SLOTS, PART, QF), bf16)] * 3,
        in_specs=[pl.BlockSpec((n, 3, PART, QF), lambda i: (i, 0, 0, 0))],
        out_specs=[part] * 3,
        cost_estimate=cost(0, 12 << 20),
        name="finish",
    )(moments)


def exchange(x):
    return lax.all_to_all(x, "expert", split_axis=0, concat_axis=0, tiled=True)


def shift(x, by):
    return lax.ppermute(x, "dp", [(i, (i + by) % N_DP) for i in range(N_DP)])


def ring(x):
    low, high = x[:HALF], x[HALF:]
    la = shift(low, 1)
    rb = shift(high, -1)
    lb = shift(high, 1)
    ra = shift(low, -1)
    fa = shift(la, 1)
    fb = shift(rb, -1)
    return (x, la, lb, ra, rb, fa, fb)


def device_step(
    tokens,
    cotangent,
    routes,
    route_weight,
    gate_weight,
    up_weight,
    down_weight,
    first_moment,
    second_moment,
    placement,
    migration_plan,
):
    index = lax.axis_index("expert").astype(jnp.int32)[None]
    dp = lax.axis_index("dp").astype(jnp.int32)[None]
    wg, wu, wd = gate_weight[0], up_weight[0], down_weight[0]
    first_rows, pos, wt = select_rows(index, placement, routes, route_weight, tokens)
    rows = (first_rows, rest_rows(pos, tokens))
    got = [exchange(x) for x in rows]
    sent_grads, high, low = scale_rows(pos, wt, cotangent)
    got_grads = exchange(sent_grads.reshape(SLOTS, CAP, QD)).reshape(ROWS, QD)
    packed = jnp.concatenate(
        [x[0].reshape(SLOTS, PART, QF) for x in (gate_weight, first_moment, second_moment)],
        axis=1,
    )
    states = exchange(packed)
    pieces = [ring(x) for x in got]
    slope, h = hidden_of(dp, pieces, wg, wu)
    carry = ()
    hg = []
    for part in range(2):
        partials = partial_grads(dp, got_grads, wd, part)
        hg.append([partials[0]] + [shift(partials[k], k) for k in range(1, N_DP)])
    for part in range(2):
        carry = (weight_grads(dp, hg[part], slope, pieces, part, carry),)
    wgrad = carry[0]
    got_wgrad = exchange(wgrad.reshape(SLOTS, PART, QF))
    moments = exchange(update(migration_plan, placement, got_wgrad, states))
    out = outputs_of(dp, [ring(h.reshape(SLOTS, CAP, QF))], wd)
    returned = exchange(out.reshape(SLOTS, CAP, QD)).reshape(ROWS, QD)
    layer_output = combine(high, low, returned)
    results = finish(moments)
    return (layer_output,) + tuple(r.reshape(1, D, QF) for r in results)


def solution(mesh):
    placed = (
        P("expert", "dp"),
        P("expert", "dp"),
        P("expert", None),
        P("expert", None),
        P("expert", None, "dp"),
        P("expert", None, "dp"),
        P("expert", None, "dp"),
        P("expert", None, "dp"),
        P("expert", None, "dp"),
        P(),
        P(),
    )
    return jax.shard_map(
        device_step,
        mesh=mesh,
        in_specs=placed,
        out_specs=(
            P("expert", "dp"),
            P("expert", None, "dp"),
            P("expert", None, "dp"),
            P("expert", None, "dp"),
        ),
        check_vma=False,
    )
```

```python
import functools
import math

import jax
import jax.numpy as jnp
from jax import lax
from jax.experimental import pallas as pl
from jax.experimental.pallas import tpu as pltpu
from jax.sharding import PartitionSpec as P


D = 3584
FF = 1024
N_DP = 4
SLOTS = 32
CAP = 48
TOK = 128
QD = D // N_DP
QF = FF // N_DP
PART = D // SLOTS
CHUNKS = ((0, 16), (16, 48))
ROWS = SLOTS * CAP
HALF = SLOTS // 2

beta_first = 0.9
beta_second = 0.95
learn_rate = 0.02
weight_decay = 0.1
epsilon = 1e-08
scale_in = 1.0 / math.sqrt(D)
scale_mid = 1.0 / math.sqrt(FF)


f32 = jnp.float32
bf16 = jnp.bfloat16
VMEM = pltpu.VMEM
SMEM = pltpu.SMEM


def vspec():
    return pl.BlockSpec(memory_space=VMEM)


def sspec():
    return pl.BlockSpec(memory_space=SMEM)


def cost(flops, nbytes):
    return pl.CostEstimate(flops=flops, transcendentals=0, bytes_accessed=nbytes)


def select_kernel(index, place, routes, weights, tokens, out, pos_out, wt_out, sel):
    me = index[0].astype(f32)
    a = lax.broadcasted_iota(jnp.int32, (SLOTS, SLOTS), 0)
    b = lax.broadcasted_iota(jnp.int32, (SLOTS, SLOTS), 1)
    row = place[...].astype(f32)
    col = jnp.sum(jnp.where(a == b, row, 0.0), axis=1, keepdims=True)
    same = jnp.where(jnp.abs(col - row) < 0.5, 1.0, 0.0)
    copies = jnp.sum(same, axis=1, keepdims=True)
    rank = jnp.sum(jnp.where(b < a, same, 0.0), axis=1, keepdims=True)
    turn = me - copies * jnp.floor((me + 0.5) / copies)
    active = jnp.abs(rank - turn) < 0.5
    hit = jnp.zeros((SLOTS, TOK), f32)
    wt = jnp.zeros((SLOTS, TOK), f32)
    for k in range(routes.shape[0]):
        match = (jnp.abs(routes[k : k + 1, :].astype(f32) - col) < 0.5) & active
        hit = hit + jnp.where(match, 1.0, 0.0)
        wt = wt + jnp.where(match, weights[k : k + 1, :], 0.0)
    t0 = lax.broadcasted_iota(jnp.int32, (TOK, TOK), 0)
    t1 = lax.broadcasted_iota(jnp.int32, (TOK, TOK), 1)
    before = jnp.where(t0 < t1, 1.0, 0.0).astype(bf16)
    pos = jnp.dot(hit.astype(bf16), before, preferred_element_type=f32)
    pos = jnp.where(hit > 0.5, pos, -1.0)
    pos_out[...] = pos
    wt_out[...] = wt
    mark_rows(pos, wt, CHUNKS[0], sel, None)
    spread_rows(CHUNKS[0], sel, tokens, out)


def mark_rows(pos, wt, chunk, sel, selw):
    lo, hi = chunk
    want = (lax.broadcasted_iota(jnp.int32, (hi - lo, TOK), 0) + lo).astype(f32)
    for j in range(SLOTS):
        chosen = jnp.abs(pos[j : j + 1, :] - want) < 0.5
        if sel is not None:
            sel[j] = jnp.where(chosen, 1.0, 0.0).astype(bf16)
        if selw is not None:
            selw[j] = jnp.where(chosen, wt[j : j + 1, :], 0.0)


def spread_rows(chunk, sel, values, out):
    rows = chunk[1] - chunk[0]
    group = 256 // rows
    for j in range(0, SLOTS, group):
        picks = sel[j : j + group].reshape(group * rows, TOK)
        got = jnp.dot(picks, values[...], preferred_element_type=f32).astype(bf16)
        out[j : j + group] = got.reshape(group, rows, QD)


def select_rows(index, placement, routes, weights, tokens):
    rows = CHUNKS[0][1]
    return pl.pallas_call(
        select_kernel,
        out_shape=[
            jax.ShapeDtypeStruct((SLOTS, rows, QD), bf16),
            jax.ShapeDtypeStruct((SLOTS, TOK), f32),
            jax.ShapeDtypeStruct((SLOTS, TOK), f32),
        ],
        in_specs=[sspec()] + [vspec()] * 4,
        out_specs=[vspec()] * 3,
        scratch_shapes=[VMEM((SLOTS, rows, TOK), bf16)],
        cost_estimate=cost(2 * ROWS * TOK * QD // 3, 2 << 20),
        name="select_rows",
    )(index, placement[None, :], routes.T, weights.T, tokens)


def rest_kernel(pos_in, tokens, out, sel):
    pos = pos_in[...]
    mark_rows(pos, None, CHUNKS[1], sel, None)
    spread_rows(CHUNKS[1], sel, tokens, out)


def rest_rows(pos, tokens):
    lo, hi = CHUNKS[1]
    return pl.pallas_call(
        rest_kernel,
        out_shape=jax.ShapeDtypeStruct((SLOTS, hi - lo, QD), bf16),
        in_specs=[vspec()] * 2,
        out_specs=vspec(),
        scratch_shapes=[VMEM((SLOTS, hi - lo, TOK), bf16)],
        cost_estimate=cost(2 * ROWS * TOK * QD, 4 << 20),
        name="rest_rows",
    )(pos, tokens)


def scale_kernel(pos_in, wt_in, cot, out, high_out, low_out, selw):
    mark_rows(pos_in[...], wt_in[...], (0, CAP), None, selw)
    group = 8
    for j in range(0, SLOTS, group):
        w = selw[j : j + group].reshape(group * CAP, TOK)
        picks = jnp.where(w != 0.0, 1.0, 0.0).astype(bf16)
        picked = jnp.dot(picks, cot[...], preferred_element_type=f32)
        rows = pl.ds(j * CAP, group * CAP)
        out[rows, :] = (jnp.sum(w, axis=1, keepdims=True) * picked).astype(bf16)
        high = w.astype(bf16)
        high_out[rows, :] = high
        low_out[rows, :] = (w - high.astype(f32)).astype(bf16)


def scale_rows(pos, wt, cot):
    return pl.pallas_call(
        scale_kernel,
        out_shape=[
            jax.ShapeDtypeStruct((ROWS, QD), bf16),
            jax.ShapeDtypeStruct((ROWS, TOK), bf16),
            jax.ShapeDtypeStruct((ROWS, TOK), bf16),
        ],
        in_specs=[vspec()] * 3,
        out_specs=[vspec()] * 3,
        scratch_shapes=[VMEM((SLOTS, CAP, TOK), f32)],
        cost_estimate=cost(2 * ROWS * TOK * QD, 4 << 20),
        name="scale_rows",
    )(pos, wt, cot)


def row_block(block, width):
    return pl.BlockSpec((block, width), lambda i: (i, 0))


def piece_specs(n, pieces):
    half = HALF // n
    specs = []
    for group in pieces:
        shape = (n,) + group[0].shape[1:]
        own = pl.BlockSpec(shape, lambda i: (i, 0, 0))
        low = pl.BlockSpec(shape, lambda i: (jnp.minimum(i, half - 1), 0, 0))
        high = pl.BlockSpec(shape, lambda i: (jnp.maximum(i - half, 0), 0, 0))
        specs += [own] + [low, high] * 3
    return specs


def whole(shape):
    return pl.BlockSpec(shape, lambda i: (0,) * len(shape))


def gather_pieces(n, dp, pieces, out):
    first = pl.program_id(0) < HALF // n
    at = 0
    for j in range(0, len(pieces), 7):
        own, la, lb, ra, rb, fa, fb = pieces[j : j + 7]
        rows, width = own.shape[1:]
        for shift, x in (
            (0, own[...]),
            (3, jnp.where(first, la[...], lb[...])),
            (1, jnp.where(first, ra[...], rb[...])),
            (2, jnp.where(first, fa[...], fb[...])),
        ):
            q = lax.rem(dp[0] + shift, N_DP)
            out[:, at : at + rows, pl.ds(pl.multiple_of(q * width, width), width)] = x
        at += rows


def flat(pieces):
    return [x for group in pieces for x in group]


HIDDEN_SOURCES = 8


def hidden_kernel(count, dp, *refs):
    pieces, (wg, wu, slope_out, h_out, gathered) = refs[:count], refs[count:]
    gather_pieces(HIDDEN_SOURCES, dp, pieces, gathered)
    x = gathered[...].reshape(HIDDEN_SOURCES * CAP, D)
    g = jnp.dot(x, wg[...], preferred_element_type=f32) * scale_in
    u = jnp.dot(x, wu[...], preferred_element_type=f32) * scale_in
    s = 1.0 / (1.0 + jnp.exp(-g))
    slope_out[...] = u * s * (1.0 + g * (1.0 - s))
    h_out[...] = (g * s * u).astype(bf16)


def hidden_of(dp, pieces, wg, wu):
    n = HIDDEN_SOURCES
    block = n * CAP
    inputs = flat(pieces)
    return pl.pallas_call(
        functools.partial(hidden_kernel, len(inputs)),
        grid=(SLOTS // n,),
        out_shape=[
            jax.ShapeDtypeStruct((ROWS, QF), f32),
            jax.ShapeDtypeStruct((ROWS, QF), bf16),
        ],
        in_specs=[sspec()] + piece_specs(n, pieces) + [whole((D, QF)), whole((D, QF))],
        out_specs=[row_block(block, QF)] * 2,
        scratch_shapes=[VMEM((n, CAP, D), bf16)],
        cost_estimate=cost(4 * ROWS * D * QF, ROWS * D * 2 + 8 * D * QF),
        name="hidden",
    )(dp, *inputs, wg, wu)


PARTIAL_BLOCK = 384


def partial_kernel(dp, x, wd, *outs):
    for k, out in enumerate(outs):
        q = lax.rem(dp[0] + k, N_DP)
        out[...] = lax.dot_general(
            x[...],
            wd[pl.ds(pl.multiple_of(q * QF, QF), QF), :],
            (((1,), (1,)), ((), ())),
            preferred_element_type=f32,
        ).astype(bf16)


def partial_grads(dp, x, wd, part):
    block = PARTIAL_BLOCK
    rows = ROWS // 2
    steps = rows // block
    return pl.pallas_call(
        partial_kernel,
        grid=(steps,),
        out_shape=[jax.ShapeDtypeStruct((rows, QF), bf16)] * N_DP,
        in_specs=[
            sspec(),
            pl.BlockSpec((block, QD), lambda i: (part * steps + i, 0)),
            whole((FF, QD)),
        ],
        out_specs=[row_block(block, QF)] * N_DP,
        cost_estimate=cost(2 * rows * QD * FF, 4 << 20),
    )(dp, x, wd)


HALF_ROWS = ROWS // 2


def weight_kernel(dp, *refs):
    sums, slope, pieces = refs[:6], refs[6], refs[7:21]
    out, x0, x1, parts, slopes, sems = refs[21:]
    count = len(sums)
    first = [pltpu.make_async_copy(r, parts.at[n], sems.at[n]) for n, r in enumerate(sums)]
    first.append(pltpu.make_async_copy(slope, slopes, sems.at[count]))
    count += 1
    by_piece = []
    for k in range(N_DP):
        copies = []
        for x, group in ((x0, pieces[:7]), (x1, pieces[7:])):
            if k == 0:
                copies.append(pltpu.make_async_copy(group[0], x.at[0], sems.at[count]))
                count += 1
                continue
            for h in range(2):
                to = x.at[k, pl.ds(HALF * h, HALF)]
                copies.append(pltpu.make_async_copy(group[2 * k - 1 + h], to, sems.at[count]))
                count += 1
        by_piece.append(copies)
    for copies in [first] + by_piece:
        for copy in copies:
            copy.start()
    for copy in first:
        copy.wait()
    gg = []
    for h in range(2):
        total = parts[h].astype(f32) + parts[2 + h].astype(f32) + parts[4 + h].astype(f32)
        total = total * scale_mid * slopes[pl.ds(HALF_ROWS * h, HALF_ROWS), :]
        gg.append(total.astype(bf16).reshape(HALF, CAP, QF))
    gg = jnp.concatenate(gg, axis=0)
    cut = CHUNKS[0][1]
    left0 = gg[:, :cut].reshape(SLOTS * cut, QF).T
    left1 = gg[:, cut:].reshape(SLOTS * (CAP - cut), QF).T
    for k, shift in enumerate((0, 3, 1, 2)):
        for copy in by_piece[k]:
            copy.wait()
        q = lax.rem(dp[0] + shift, N_DP)
        product = jnp.dot(left0, x0[k].reshape(-1, QD), preferred_element_type=f32)
        product = product + jnp.dot(left1, x1[k].reshape(-1, QD), preferred_element_type=f32)
        to = pl.ds(pl.multiple_of(q * QD, QD), QD)
        out[to, :] = (product * scale_in).astype(bf16).T


def weight_grads(dp, sums, slope, pieces):
    inputs = [*sums, slope, *flat(pieces)]
    return pl.pallas_call(
        weight_kernel,
        out_shape=jax.ShapeDtypeStruct((D, QF), bf16),
        in_specs=[sspec()] + [pl.BlockSpec(memory_space=pl.ANY)] * len(inputs),
        out_specs=vspec(),
        scratch_shapes=[
            *[VMEM((N_DP, SLOTS, hi - lo, QD), bf16) for lo, hi in CHUNKS],
            VMEM((len(sums), HALF_ROWS, QF), bf16),
            VMEM((ROWS, QF), f32),
            pltpu.SemaphoreType.DMA((len(inputs),)),
        ],
        cost_estimate=cost(2 * ROWS * D * QF, ROWS * D * 2 + (4 << 20)),
        name="weight_grads",
    )(dp, *inputs)


def add_kernel(a, b, c, d, low, high):
    low[...] = (a[...].astype(f32) + b[...].astype(f32)).astype(bf16)
    high[...] = (c[...].astype(f32) + d[...].astype(f32)).astype(bf16)


def add_pairs(*arrays):
    return pl.pallas_call(
        add_kernel,
        out_shape=[jax.ShapeDtypeStruct((HALF_ROWS, QF), bf16)] * 2,
        in_specs=[vspec()] * 4,
        out_specs=[vspec()] * 2,
        cost_estimate=cost(2 * HALF_ROWS * QF, 3 << 20),
        name="add_pairs",
    )(*arrays)


OUTPUT_SOURCES = 8


def output_kernel(count, dp, *refs):
    pieces, (wd, out, gathered) = refs[:count], refs[count:]
    gather_pieces(OUTPUT_SOURCES, dp, pieces, gathered)
    x = gathered[...].reshape(OUTPUT_SOURCES * CAP, FF)
    total = jnp.dot(x, wd[...], preferred_element_type=f32)
    out[...] = (total * scale_mid).astype(bf16)


def outputs_of(dp, pieces, wd):
    n = OUTPUT_SOURCES
    inputs = flat(pieces)
    return pl.pallas_call(
        functools.partial(output_kernel, len(inputs)),
        grid=(SLOTS // n,),
        out_shape=jax.ShapeDtypeStruct((ROWS, QD), bf16),
        in_specs=[sspec()] + piece_specs(n, pieces) + [whole((FF, QD))],
        out_specs=row_block(n * CAP, QD),
        scratch_shapes=[VMEM((n, CAP, FF), bf16)],
        cost_estimate=cost(2 * ROWS * FF * QD, ROWS * (FF + QD) * 2),
        name="outputs",
    )(dp, *inputs, wd)


def combine_kernel(high, low, rows, out):
    total = jnp.zeros(out.shape, f32)
    for part in (high, low):
        total = total + lax.dot_general(
            part[...], rows[...], (((0,), (0,)), ((), ())), preferred_element_type=f32
        )
    out[...] = total.astype(bf16)


def combine(high, low, rows):
    return pl.pallas_call(
        combine_kernel,
        out_shape=jax.ShapeDtypeStruct((TOK, QD), bf16),
        in_specs=[vspec()] * 3,
        out_specs=vspec(),
        cost_estimate=cost(4 * ROWS * TOK * QD, 4 << 20),
        name="combine",
    )(high, low, rows)


UPDATE_ROWS = 16


def update_kernel(plan, placement, grads, gate, first, second, out, total):
    total[...] = jnp.zeros_like(total)
    for s in range(SLOTS):
        total[placement[s]] += grads[s].astype(f32)

    def body(s, carry):
        p = plan[s]
        g = total[placement[p]]
        one = beta_first * first[p].astype(f32) + (1.0 - beta_first) * g
        two = beta_second * second[p].astype(f32) + (1.0 - beta_second) * g * g
        kept = gate[p].astype(f32) * (1.0 - learn_rate * weight_decay)
        out[s, 0] = (kept - learn_rate * one / (jnp.sqrt(two) + epsilon)).astype(bf16)
        out[s, 1] = one.astype(bf16)
        out[s, 2] = two.astype(bf16)
        return carry

    lax.fori_loop(0, SLOTS, body, 0, unroll=4)


def update(plan, placement, grads, states):
    steps = PART // UPDATE_ROWS

    def part(n):
        return pl.BlockSpec((SLOTS, UPDATE_ROWS, QF), lambda i, *_: (0, n * steps + i, 0))

    return pl.pallas_call(
        update_kernel,
        grid_spec=pltpu.PrefetchScalarGridSpec(
            num_scalar_prefetch=2,
            grid=(steps,),
            in_specs=[part(0), part(0), part(1), part(2)],
            out_specs=pl.BlockSpec((SLOTS, 3, UPDATE_ROWS, QF), lambda i, *_: (0, 0, i, 0)),
            scratch_shapes=[VMEM((SLOTS, UPDATE_ROWS, QF), f32)],
        ),
        out_shape=jax.ShapeDtypeStruct((SLOTS, 3, PART, QF), bf16),
        cost_estimate=cost(20 * D * SLOTS * QF // SLOTS, 10 << 20),
        name="update",
    )(plan, placement, grads, states, states, states)


def finish_kernel(moments, *outs):
    for k, out in enumerate(outs):
        out[...] = moments[:, k]


def finish(moments):
    n = 8
    part = pl.BlockSpec((n, PART, QF), lambda i: (i, 0, 0))
    return pl.pallas_call(
        finish_kernel,
        grid=(SLOTS // n,),
        out_shape=[jax.ShapeDtypeStruct((SLOTS, PART, QF), bf16)] * 3,
        in_specs=[pl.BlockSpec((n, 3, PART, QF), lambda i: (i, 0, 0, 0))],
        out_specs=[part] * 3,
        cost_estimate=cost(0, 12 << 20),
        name="finish",
    )(moments)


def exchange(x):
    return lax.all_to_all(x, "expert", split_axis=0, concat_axis=0, tiled=True)


def shift(x, by):
    return lax.ppermute(x, "dp", [(i, (i + by) % N_DP) for i in range(N_DP)])


def ring(x):
    low, high = x[:HALF], x[HALF:]
    la = shift(low, 1)
    rb = shift(high, -1)
    lb = shift(high, 1)
    ra = shift(low, -1)
    fa = shift(la, 1)
    fb = shift(rb, -1)
    return (x, la, lb, ra, rb, fa, fb)


def device_step(
    tokens,
    cotangent,
    routes,
    route_weight,
    gate_weight,
    up_weight,
    down_weight,
    first_moment,
    second_moment,
    placement,
    migration_plan,
):
    index = lax.axis_index("expert").astype(jnp.int32)[None]
    dp = lax.axis_index("dp").astype(jnp.int32)[None]
    wg, wu, wd = gate_weight[0], up_weight[0], down_weight[0]
    first_rows, pos, wt = select_rows(index, placement, routes, route_weight, tokens)
    rows = (first_rows, rest_rows(pos, tokens))
    got = [exchange(x) for x in rows]
    sent_grads, weight_high, weight_low = scale_rows(pos, wt, cotangent)
    got_grads = exchange(sent_grads.reshape(SLOTS, CAP, QD)).reshape(ROWS, QD)
    packed = jnp.concatenate(
        [x[0].reshape(SLOTS, PART, QF) for x in (gate_weight, first_moment, second_moment)],
        axis=1,
    )
    states = exchange(packed)
    pieces = [ring(x) for x in got]
    slope, h = hidden_of(dp, pieces, wg, wu)
    low = partial_grads(dp, got_grads, wd, 0)
    high = partial_grads(dp, got_grads, wd, 1)
    far_low = shift(low[2], 1)
    far_high = shift(high[2], -1)
    near_low = shift(low[3], -1)
    near_high = shift(high[1], 1)
    pair_low, pair_high = add_pairs(low[1], far_low, high[3], far_high)
    pair_low = shift(pair_low, 1)
    pair_high = shift(pair_high, -1)
    sums = (low[0], high[0], near_low, near_high, pair_low, pair_high)
    wgrad = weight_grads(dp, sums, slope, pieces)
    got_wgrad = exchange(wgrad.reshape(SLOTS, PART, QF))
    moments = exchange(update(migration_plan, placement, got_wgrad, states))
    out = outputs_of(dp, [ring(h.reshape(SLOTS, CAP, QF))], wd)
    returned = exchange(out.reshape(SLOTS, CAP, QD)).reshape(ROWS, QD)
    layer_output = combine(weight_high, weight_low, returned)
    results = finish(moments)
    return (layer_output,) + tuple(r.reshape(1, D, QF) for r in results)


def solution(mesh):
    placed = (
        P("expert", "dp"),
        P("expert", "dp"),
        P("expert", None),
        P("expert", None),
        P("expert", None, "dp"),
        P("expert", None, "dp"),
        P("expert", None, "dp"),
        P("expert", None, "dp"),
        P("expert", None, "dp"),
        P(),
        P(),
    )
    return jax.shard_map(
        device_step,
        mesh=mesh,
        in_specs=placed,
        out_specs=(
            P("expert", "dp"),
            P("expert", None, "dp"),
            P("expert", None, "dp"),
            P("expert", None, "dp"),
        ),
        check_vma=False,
    )
```

```python
import functools
import math

import jax
import jax.numpy as jnp
from jax import lax
from jax.experimental import pallas as pl
from jax.experimental.pallas import tpu as pltpu
from jax.sharding import PartitionSpec as P


D = 3584
FF = 1024
N_DP = 4
SLOTS = 32
CAP = 48
TOK = 128
QD = D // N_DP
QF = FF // N_DP
PART = D // SLOTS
CHUNKS = ((0, 16), (16, 48))
ROWS = SLOTS * CAP
HALF = SLOTS // 2

beta_first = 0.9
beta_second = 0.95
learn_rate = 0.02
weight_decay = 0.1
epsilon = 1e-08
scale_in = 1.0 / math.sqrt(D)
scale_mid = 1.0 / math.sqrt(FF)


f32 = jnp.float32
bf16 = jnp.bfloat16
VMEM = pltpu.VMEM
SMEM = pltpu.SMEM


def vspec():
    return pl.BlockSpec(memory_space=VMEM)


def sspec():
    return pl.BlockSpec(memory_space=SMEM)


def cost(flops, nbytes):
    return pl.CostEstimate(flops=flops, transcendentals=0, bytes_accessed=nbytes)


def select_kernel(index, place, routes, weights, tokens, out, pos_out, wt_out, sel):
    me = index[0].astype(f32)
    a = lax.broadcasted_iota(jnp.int32, (SLOTS, SLOTS), 0)
    b = lax.broadcasted_iota(jnp.int32, (SLOTS, SLOTS), 1)
    row = place[...].astype(f32)
    col = jnp.sum(jnp.where(a == b, row, 0.0), axis=1, keepdims=True)
    same = jnp.where(jnp.abs(col - row) < 0.5, 1.0, 0.0)
    copies = jnp.sum(same, axis=1, keepdims=True)
    rank = jnp.sum(jnp.where(b < a, same, 0.0), axis=1, keepdims=True)
    turn = me - copies * jnp.floor((me + 0.5) / copies)
    active = jnp.abs(rank - turn) < 0.5
    hit = jnp.zeros((SLOTS, TOK), f32)
    wt = jnp.zeros((SLOTS, TOK), f32)
    for k in range(routes.shape[0]):
        match = (jnp.abs(routes[k : k + 1, :].astype(f32) - col) < 0.5) & active
        hit = hit + jnp.where(match, 1.0, 0.0)
        wt = wt + jnp.where(match, weights[k : k + 1, :], 0.0)
    t0 = lax.broadcasted_iota(jnp.int32, (TOK, TOK), 0)
    t1 = lax.broadcasted_iota(jnp.int32, (TOK, TOK), 1)
    before = jnp.where(t0 < t1, 1.0, 0.0).astype(bf16)
    pos = jnp.dot(hit.astype(bf16), before, preferred_element_type=f32)
    pos = jnp.where(hit > 0.5, pos, -1.0)
    pos_out[...] = pos
    wt_out[...] = wt
    mark_rows(pos, wt, CHUNKS[0], sel, None)
    spread_rows(CHUNKS[0], sel, tokens, out)


def mark_rows(pos, wt, chunk, sel, selw):
    lo, hi = chunk
    want = (lax.broadcasted_iota(jnp.int32, (hi - lo, TOK), 0) + lo).astype(f32)
    for j in range(SLOTS):
        chosen = jnp.abs(pos[j : j + 1, :] - want) < 0.5
        if sel is not None:
            sel[j] = jnp.where(chosen, 1.0, 0.0).astype(bf16)
        if selw is not None:
            selw[j] = jnp.where(chosen, wt[j : j + 1, :], 0.0)


def spread_rows(chunk, sel, values, out):
    rows = chunk[1] - chunk[0]
    group = 256 // rows
    for j in range(0, SLOTS, group):
        picks = sel[j : j + group].reshape(group * rows, TOK)
        got = jnp.dot(picks, values[...], preferred_element_type=f32).astype(bf16)
        out[j : j + group] = got.reshape(group, rows, QD)


def select_rows(index, placement, routes, weights, tokens):
    rows = CHUNKS[0][1]
    return pl.pallas_call(
        select_kernel,
        out_shape=[
            jax.ShapeDtypeStruct((SLOTS, rows, QD), bf16),
            jax.ShapeDtypeStruct((SLOTS, TOK), f32),
            jax.ShapeDtypeStruct((SLOTS, TOK), f32),
        ],
        in_specs=[sspec()] + [vspec()] * 4,
        out_specs=[vspec()] * 3,
        scratch_shapes=[VMEM((SLOTS, rows, TOK), bf16)],
        cost_estimate=cost(2 * ROWS * TOK * QD // 3, 2 << 20),
        name="select_rows",
    )(index, placement[None, :], routes.T, weights.T, tokens)


def rest_kernel(pos_in, tokens, out, sel):
    pos = pos_in[...]
    mark_rows(pos, None, CHUNKS[1], sel, None)
    spread_rows(CHUNKS[1], sel, tokens, out)


def rest_rows(pos, tokens):
    lo, hi = CHUNKS[1]
    return pl.pallas_call(
        rest_kernel,
        out_shape=jax.ShapeDtypeStruct((SLOTS, hi - lo, QD), bf16),
        in_specs=[vspec()] * 2,
        out_specs=vspec(),
        scratch_shapes=[VMEM((SLOTS, hi - lo, TOK), bf16)],
        cost_estimate=cost(2 * ROWS * TOK * QD, 4 << 20),
        name="rest_rows",
    )(pos, tokens)


def scale_kernel(pos_in, wt_in, cot, out, high_out, low_out, selw):
    mark_rows(pos_in[...], wt_in[...], (0, CAP), None, selw)
    group = 8
    for j in range(0, SLOTS, group):
        w = selw[j : j + group].reshape(group * CAP, TOK)
        picks = jnp.where(w != 0.0, 1.0, 0.0).astype(bf16)
        picked = jnp.dot(picks, cot[...], preferred_element_type=f32)
        rows = pl.ds(j * CAP, group * CAP)
        out[rows, :] = (jnp.sum(w, axis=1, keepdims=True) * picked).astype(bf16)
        high = w.astype(bf16)
        high_out[rows, :] = high
        low_out[rows, :] = (w - high.astype(f32)).astype(bf16)


def scale_rows(pos, wt, cot):
    return pl.pallas_call(
        scale_kernel,
        out_shape=[
            jax.ShapeDtypeStruct((ROWS, QD), bf16),
            jax.ShapeDtypeStruct((ROWS, TOK), bf16),
            jax.ShapeDtypeStruct((ROWS, TOK), bf16),
        ],
        in_specs=[vspec()] * 3,
        out_specs=[vspec()] * 3,
        scratch_shapes=[VMEM((SLOTS, CAP, TOK), f32)],
        cost_estimate=cost(2 * ROWS * TOK * QD, 4 << 20),
        name="scale_rows",
    )(pos, wt, cot)


def row_block(block, width):
    return pl.BlockSpec((block, width), lambda i: (i, 0))


def half_of(n, pieces, part):
    inputs, specs = [], []
    for own, la, lb, ra, rb, fa, fb in pieces:
        shape = (n,) + own.shape[1:]
        inputs += [own] + ([la, ra, fa] if part == 0 else [lb, rb, fb])
        specs += [pl.BlockSpec(shape, lambda i: (part * (HALF // n) + i, 0, 0))]
        specs += [pl.BlockSpec(shape, lambda i: (i, 0, 0))] * 3
    return inputs, specs


def whole(shape):
    return pl.BlockSpec(shape, lambda i: (0,) * len(shape))


def flat(pieces):
    return [x for group in pieces for x in group]


HIDDEN_SOURCES = 8


def hidden_kernel(count, dp, *refs):
    pieces, (wg, wu, slope_out, h_out, gathered) = refs[:count], refs[count:]
    at = 0
    for j in range(0, count, N_DP):
        rows = pieces[j].shape[1]
        for shift, ref in zip((0, 3, 1, 2), pieces[j : j + N_DP]):
            q = lax.rem(dp[0] + shift, N_DP)
            gathered[:, at : at + rows, pl.ds(pl.multiple_of(q * QD, QD), QD)] = ref[...]
        at += rows
    x = gathered[...].reshape(HIDDEN_SOURCES * CAP, D)
    g = jnp.dot(x, wg[...], preferred_element_type=f32) * scale_in
    u = jnp.dot(x, wu[...], preferred_element_type=f32) * scale_in
    s = 1.0 / (1.0 + jnp.exp(-g))
    slope_out[...] = u * s * (1.0 + g * (1.0 - s))
    h_out[...] = (g * s * u).astype(bf16)


def hidden_of(dp, pieces, wg, wu, part):
    n = HIDDEN_SOURCES
    block = n * CAP
    rows = ROWS // 2
    inputs, specs = half_of(n, pieces, part)
    return pl.pallas_call(
        functools.partial(hidden_kernel, len(inputs)),
        grid=(HALF // n,),
        out_shape=[
            jax.ShapeDtypeStruct((rows, QF), f32),
            jax.ShapeDtypeStruct((rows, QF), bf16),
        ],
        in_specs=[sspec()] + specs + [whole((D, QF)), whole((D, QF))],
        out_specs=[row_block(block, QF)] * 2,
        scratch_shapes=[VMEM((n, CAP, D), bf16)],
        cost_estimate=cost(4 * rows * D * QF, rows * D * 2 + 8 * D * QF),
    )(dp, *inputs, wg, wu)


PARTIAL_BLOCK = 384


def partial_kernel(dp, x, wd, *outs):
    for k, out in enumerate(outs):
        q = lax.rem(dp[0] + k, N_DP)
        out[...] = lax.dot_general(
            x[...],
            wd[pl.ds(pl.multiple_of(q * QF, QF), QF), :],
            (((1,), (1,)), ((), ())),
            preferred_element_type=f32,
        ).astype(bf16)


def partial_grads(dp, x, wd, part):
    block = PARTIAL_BLOCK
    rows = ROWS // 2
    steps = rows // block
    return pl.pallas_call(
        partial_kernel,
        grid=(steps,),
        out_shape=[jax.ShapeDtypeStruct((rows, QF), bf16)] * N_DP,
        in_specs=[
            sspec(),
            pl.BlockSpec((block, QD), lambda i: (part * steps + i, 0)),
            whole((FF, QD)),
        ],
        out_specs=[row_block(block, QF)] * N_DP,
        cost_estimate=cost(2 * rows * QD * FF, 4 << 20),
    )(dp, x, wd)


HALF_ROWS = ROWS // 2


def weight_kernel(dp, *refs):
    sums, slope, pieces = refs[:6], refs[6:8], refs[8:22]
    out, x0, x1, parts, slopes, sems = refs[22:]
    count = len(sums)
    first = [pltpu.make_async_copy(r, parts.at[n], sems.at[n]) for n, r in enumerate(sums)]
    for h, ref in enumerate(slope):
        first.append(pltpu.make_async_copy(ref, slopes.at[h], sems.at[count]))
        count += 1
    by_piece = []
    for k in range(N_DP):
        copies = []
        for x, group in ((x0, pieces[:7]), (x1, pieces[7:])):
            if k == 0:
                copies.append(pltpu.make_async_copy(group[0], x.at[0], sems.at[count]))
                count += 1
                continue
            for h in range(2):
                to = x.at[k, pl.ds(HALF * h, HALF)]
                copies.append(pltpu.make_async_copy(group[2 * k - 1 + h], to, sems.at[count]))
                count += 1
        by_piece.append(copies)
    for copies in [first] + by_piece:
        for copy in copies:
            copy.start()
    for copy in first:
        copy.wait()
    gg = []
    for h in range(2):
        total = parts[h].astype(f32) + parts[2 + h].astype(f32) + parts[4 + h].astype(f32)
        total = total * scale_mid * slopes[h]
        gg.append(total.astype(bf16).reshape(HALF, CAP, QF))
    gg = jnp.concatenate(gg, axis=0)
    cut = CHUNKS[0][1]
    left0 = gg[:, :cut].reshape(SLOTS * cut, QF).T
    left1 = gg[:, cut:].reshape(SLOTS * (CAP - cut), QF).T
    for k, shift in enumerate((0, 3, 1, 2)):
        for copy in by_piece[k]:
            copy.wait()
        q = lax.rem(dp[0] + shift, N_DP)
        product = jnp.dot(left0, x0[k].reshape(-1, QD), preferred_element_type=f32)
        product = product + jnp.dot(left1, x1[k].reshape(-1, QD), preferred_element_type=f32)
        to = pl.ds(pl.multiple_of(q * QD, QD), QD)
        out[to, :] = (product * scale_in).astype(bf16).T


def weight_grads(dp, sums, slope, pieces):
    inputs = [*sums, *slope, *flat(pieces)]
    return pl.pallas_call(
        weight_kernel,
        out_shape=jax.ShapeDtypeStruct((D, QF), bf16),
        in_specs=[sspec()] + [pl.BlockSpec(memory_space=pl.ANY)] * len(inputs),
        out_specs=vspec(),
        scratch_shapes=[
            *[VMEM((N_DP, SLOTS, hi - lo, QD), bf16) for lo, hi in CHUNKS],
            VMEM((len(sums), HALF_ROWS, QF), bf16),
            VMEM((2, HALF_ROWS, QF), f32),
            pltpu.SemaphoreType.DMA((len(inputs),)),
        ],
        cost_estimate=cost(2 * ROWS * D * QF, ROWS * D * 2 + (4 << 20)),
        name="weight_grads",
    )(dp, *inputs)


def add_kernel(a, b, c, d, low, high):
    low[...] = (a[...].astype(f32) + b[...].astype(f32)).astype(bf16)
    high[...] = (c[...].astype(f32) + d[...].astype(f32)).astype(bf16)


def add_pairs(*arrays):
    return pl.pallas_call(
        add_kernel,
        out_shape=[jax.ShapeDtypeStruct((HALF_ROWS, QF), bf16)] * 2,
        in_specs=[vspec()] * 4,
        out_specs=[vspec()] * 2,
        cost_estimate=cost(2 * HALF_ROWS * QF, 3 << 20),
        name="add_pairs",
    )(*arrays)


OUTPUT_SOURCES = 8


def output_kernel(count, dp, *refs):
    pieces, (wd, out, gathered) = refs[:count], refs[count:]
    first = pl.program_id(0) < HALF // OUTPUT_SOURCES
    for j, shift in zip(range(0, count, 2), (0, 3, 1, 2)):
        q = lax.rem(dp[0] + shift, N_DP)
        to = pl.ds(pl.multiple_of(q * QF, QF), QF)
        gathered[:, :, to] = jnp.where(first, pieces[j][...], pieces[j + 1][...])
    x = gathered[...].reshape(OUTPUT_SOURCES * CAP, FF)
    total = jnp.dot(x, wd[...], preferred_element_type=f32)
    out[...] = (total * scale_mid).astype(bf16)


def outputs_of(dp, pieces, wd):
    n = OUTPUT_SOURCES
    half = HALF // n
    shape = (n, CAP, QF)
    low = pl.BlockSpec(shape, lambda i: (jnp.minimum(i, half - 1), 0, 0))
    high = pl.BlockSpec(shape, lambda i: (jnp.maximum(i - half, 0), 0, 0))
    return pl.pallas_call(
        functools.partial(output_kernel, len(pieces)),
        grid=(SLOTS // n,),
        out_shape=jax.ShapeDtypeStruct((ROWS, QD), bf16),
        in_specs=[sspec()] + [low, high] * N_DP + [whole((FF, QD))],
        out_specs=row_block(n * CAP, QD),
        scratch_shapes=[VMEM((n, CAP, FF), bf16)],
        cost_estimate=cost(2 * ROWS * FF * QD, ROWS * (FF + QD) * 2),
        name="outputs",
    )(dp, *pieces, wd)


def combine(high, low, rows):
    total = None
    for part in (high, low):
        one = lax.dot_general(part, rows, (((0,), (0,)), ((), ())), preferred_element_type=f32)
        total = one if total is None else total + one
    return total.astype(bf16)


UPDATE_ROWS = 16


def update_kernel(plan, placement, grads, gate, first, second, out, total):
    total[...] = jnp.zeros_like(total)
    for s in range(SLOTS):
        total[placement[s]] += grads[s].astype(f32)

    def body(s, carry):
        p = plan[s]
        g = total[placement[p]]
        one = beta_first * first[p].astype(f32) + (1.0 - beta_first) * g
        two = beta_second * second[p].astype(f32) + (1.0 - beta_second) * g * g
        kept = gate[p].astype(f32) * (1.0 - learn_rate * weight_decay)
        out[s, 0] = (kept - learn_rate * one / (jnp.sqrt(two) + epsilon)).astype(bf16)
        out[s, 1] = one.astype(bf16)
        out[s, 2] = two.astype(bf16)
        return carry

    lax.fori_loop(0, SLOTS, body, 0, unroll=4)


def update(plan, placement, grads, states):
    steps = PART // UPDATE_ROWS

    def part(n):
        return pl.BlockSpec((SLOTS, UPDATE_ROWS, QF), lambda i, *_: (0, n * steps + i, 0))

    return pl.pallas_call(
        update_kernel,
        grid_spec=pltpu.PrefetchScalarGridSpec(
            num_scalar_prefetch=2,
            grid=(steps,),
            in_specs=[part(0), part(0), part(1), part(2)],
            out_specs=pl.BlockSpec((SLOTS, 3, UPDATE_ROWS, QF), lambda i, *_: (0, 0, i, 0)),
            scratch_shapes=[VMEM((SLOTS, UPDATE_ROWS, QF), f32)],
        ),
        out_shape=jax.ShapeDtypeStruct((SLOTS, 3, PART, QF), bf16),
        cost_estimate=cost(20 * D * SLOTS * QF // SLOTS, 10 << 20),
        name="update",
    )(plan, placement, grads, states, states, states)


def finish_kernel(moments, *outs):
    for k, out in enumerate(outs):
        out[...] = moments[:, k]


def finish(moments):
    n = 16
    part = pl.BlockSpec((n, PART, QF), lambda i: (i, 0, 0))
    return pl.pallas_call(
        finish_kernel,
        grid=(SLOTS // n,),
        out_shape=[jax.ShapeDtypeStruct((SLOTS, PART, QF), bf16)] * 3,
        in_specs=[pl.BlockSpec((n, 3, PART, QF), lambda i: (i, 0, 0, 0))],
        out_specs=[part] * 3,
        cost_estimate=cost(0, 12 << 20),
        name="finish",
    )(moments)


def exchange(x):
    return lax.all_to_all(x, "expert", split_axis=0, concat_axis=0, tiled=True)


def shift(x, by):
    return lax.ppermute(x, "dp", [(i, (i + by) % N_DP) for i in range(N_DP)])


def ring(low, high):
    la = shift(low, 1)
    rb = shift(high, -1)
    lb = shift(high, 1)
    ra = shift(low, -1)
    fa = shift(la, 1)
    fb = shift(rb, -1)
    return (la, lb, ra, rb, fa, fb)


def device_step(
    tokens,
    cotangent,
    routes,
    route_weight,
    gate_weight,
    up_weight,
    down_weight,
    first_moment,
    second_moment,
    placement,
    migration_plan,
):
    index = lax.axis_index("expert").astype(jnp.int32)[None]
    dp = lax.axis_index("dp").astype(jnp.int32)[None]
    wg, wu, wd = gate_weight[0], up_weight[0], down_weight[0]
    first_rows, pos, wt = select_rows(index, placement, routes, route_weight, tokens)
    rows = (first_rows, rest_rows(pos, tokens))
    got = [exchange(x) for x in rows]
    sent_grads, weight_high, weight_low = scale_rows(pos, wt, cotangent)
    got_grads = exchange(sent_grads.reshape(SLOTS, CAP, QD)).reshape(ROWS, QD)
    packed = jnp.concatenate(
        [x[0].reshape(SLOTS, PART, QF) for x in (gate_weight, first_moment, second_moment)],
        axis=1,
    )
    states = exchange(packed)
    pieces = [(x, *ring(x[:HALF], x[HALF:])) for x in got]
    slope, h = zip(*[hidden_of(dp, pieces, wg, wu, part) for part in range(2)])
    low = partial_grads(dp, got_grads, wd, 0)
    high = partial_grads(dp, got_grads, wd, 1)
    far_low = shift(low[2], 1)
    far_high = shift(high[2], -1)
    near_low = shift(low[3], -1)
    near_high = shift(high[1], 1)
    pair_low, pair_high = add_pairs(low[1], far_low, high[3], far_high)
    pair_low = shift(pair_low, 1)
    pair_high = shift(pair_high, -1)
    sums = (low[0], high[0], near_low, near_high, pair_low, pair_high)
    wgrad = weight_grads(dp, sums, slope, pieces)
    got_wgrad = exchange(wgrad.reshape(SLOTS, PART, QF))
    moments = exchange(update(migration_plan, placement, got_wgrad, states))
    h = [x.reshape(HALF, CAP, QF) for x in h]
    out = outputs_of(dp, (*h, *ring(*h)), wd)
    returned = exchange(out.reshape(SLOTS, CAP, QD)).reshape(ROWS, QD)
    layer_output = combine(weight_high, weight_low, returned)
    results = finish(moments)
    return (layer_output,) + tuple(r.reshape(1, D, QF) for r in results)


def solution(mesh):
    placed = (
        P("expert", "dp"),
        P("expert", "dp"),
        P("expert", None),
        P("expert", None),
        P("expert", None, "dp"),
        P("expert", None, "dp"),
        P("expert", None, "dp"),
        P("expert", None, "dp"),
        P("expert", None, "dp"),
        P(),
        P(),
    )
    return jax.shard_map(
        device_step,
        mesh=mesh,
        in_specs=placed,
        out_specs=(
            P("expert", "dp"),
            P("expert", None, "dp"),
            P("expert", None, "dp"),
            P("expert", None, "dp"),
        ),
        check_vma=False,
    )
```

```python
import functools
import math

import jax
import jax.numpy as jnp
from jax import lax
from jax.experimental import pallas as pl
from jax.experimental.pallas import tpu as pltpu
from jax.sharding import PartitionSpec as P


D = 3584
FF = 1024
N_DP = 4
SLOTS = 32
CAP = 48
TOK = 128
QD = D // N_DP
QF = FF // N_DP
PART = D // SLOTS
CHUNKS = ((0, 32), (32, 48))
REST = CHUNKS[1][1] - CHUNKS[1][0]
ROWS = SLOTS * CAP
HALF = SLOTS // 2

beta_first = 0.9
beta_second = 0.95
learn_rate = 0.02
weight_decay = 0.1
epsilon = 1e-08
scale_in = 1.0 / math.sqrt(D)
scale_mid = 1.0 / math.sqrt(FF)


f32 = jnp.float32
bf16 = jnp.bfloat16
VMEM = pltpu.VMEM
SMEM = pltpu.SMEM


def vspec():
    return pl.BlockSpec(memory_space=VMEM)


def sspec():
    return pl.BlockSpec(memory_space=SMEM)


def cost(flops, nbytes):
    return pl.CostEstimate(flops=flops, transcendentals=0, bytes_accessed=nbytes)


def select_kernel(index, place, routes, weights, tokens, out, pos_out, wt_out, sel):
    me = index[0].astype(f32)
    a = lax.broadcasted_iota(jnp.int32, (SLOTS, SLOTS), 0)
    b = lax.broadcasted_iota(jnp.int32, (SLOTS, SLOTS), 1)
    row = place[...].astype(f32)
    col = jnp.sum(jnp.where(a == b, row, 0.0), axis=1, keepdims=True)
    same = jnp.where(jnp.abs(col - row) < 0.5, 1.0, 0.0)
    copies = jnp.sum(same, axis=1, keepdims=True)
    rank = jnp.sum(jnp.where(b < a, same, 0.0), axis=1, keepdims=True)
    turn = me - copies * jnp.floor((me + 0.5) / copies)
    active = jnp.abs(rank - turn) < 0.5
    hit = jnp.zeros((SLOTS, TOK), f32)
    wt = jnp.zeros((SLOTS, TOK), f32)
    for k in range(routes.shape[0]):
        match = (jnp.abs(routes[k : k + 1, :].astype(f32) - col) < 0.5) & active
        hit = hit + jnp.where(match, 1.0, 0.0)
        wt = wt + jnp.where(match, weights[k : k + 1, :], 0.0)
    t0 = lax.broadcasted_iota(jnp.int32, (TOK, TOK), 0)
    t1 = lax.broadcasted_iota(jnp.int32, (TOK, TOK), 1)
    before = jnp.where(t0 < t1, 1.0, 0.0).astype(bf16)
    pos = jnp.dot(hit.astype(bf16), before, preferred_element_type=f32)
    pos = jnp.where(hit > 0.5, pos, -1.0)
    pos_out[...] = pos
    wt_out[...] = wt
    mark_rows(pos, wt, CHUNKS[0], sel, None)
    spread_rows(CHUNKS[0], sel, tokens, out)


def mark_rows(pos, wt, chunk, sel, selw):
    lo, hi = chunk
    want = (lax.broadcasted_iota(jnp.int32, (hi - lo, TOK), 0) + lo).astype(f32)
    for j in range(SLOTS):
        chosen = jnp.abs(pos[j : j + 1, :] - want) < 0.5
        if sel is not None:
            sel[j] = jnp.where(chosen, 1.0, 0.0).astype(bf16)
        if selw is not None:
            selw[j] = jnp.where(chosen, wt[j : j + 1, :], 0.0)


def spread_rows(chunk, sel, values, out):
    rows = chunk[1] - chunk[0]
    group = 256 // rows
    for j in range(0, SLOTS, group):
        picks = sel[j : j + group].reshape(group * rows, TOK)
        got = jnp.dot(picks, values[...], preferred_element_type=f32).astype(bf16)
        out[j : j + group] = got.reshape(group, rows, QD)


def select_rows(index, placement, routes, weights, tokens):
    rows = CHUNKS[0][1]
    return pl.pallas_call(
        select_kernel,
        out_shape=[
            jax.ShapeDtypeStruct((SLOTS, rows, QD), bf16),
            jax.ShapeDtypeStruct((SLOTS, TOK), f32),
            jax.ShapeDtypeStruct((SLOTS, TOK), f32),
        ],
        in_specs=[sspec()] + [vspec()] * 4,
        out_specs=[vspec()] * 3,
        scratch_shapes=[VMEM((SLOTS, rows, TOK), bf16)],
        cost_estimate=cost(2 * ROWS * TOK * QD // 3, 2 << 20),
        name="select_rows",
    )(index, placement[None, :], routes.T, weights.T, tokens)


def mixed_kernel(pos_in, wt_in, tokens, cot, out, high_out, low_out, sel, selw):
    pos = pos_in[...]
    mark_rows(pos, None, CHUNKS[1], sel, None)
    mark_rows(pos, wt_in[...], (0, CAP), None, selw)
    group = 8
    for j in range(0, SLOTS, group):
        picks = sel[j : j + group].reshape(group * REST, TOK)
        got = jnp.dot(picks, tokens[...], preferred_element_type=f32).astype(bf16)
        out[j : j + group, :REST] = got.reshape(group, REST, QD)
        w = selw[j : j + group].reshape(group * CAP, TOK)
        picks = jnp.where(w != 0.0, 1.0, 0.0).astype(bf16)
        picked = jnp.dot(picks, cot[...], preferred_element_type=f32)
        scaled = (jnp.sum(w, axis=1, keepdims=True) * picked).astype(bf16)
        out[j : j + group, REST:] = scaled.reshape(group, CAP, QD)
        rows = pl.ds(j * CAP, group * CAP)
        high = w.astype(bf16)
        high_out[rows, :] = high
        low_out[rows, :] = (w - high.astype(f32)).astype(bf16)


def mixed_rows(pos, wt, tokens, cot):
    return pl.pallas_call(
        mixed_kernel,
        out_shape=[
            jax.ShapeDtypeStruct((SLOTS, REST + CAP, QD), bf16),
            jax.ShapeDtypeStruct((ROWS, TOK), bf16),
            jax.ShapeDtypeStruct((ROWS, TOK), bf16),
        ],
        in_specs=[vspec()] * 4,
        out_specs=[vspec()] * 3,
        scratch_shapes=[VMEM((SLOTS, REST, TOK), bf16), VMEM((SLOTS, CAP, TOK), f32)],
        cost_estimate=cost(3 * ROWS * TOK * QD, 5 << 20),
        name="mixed_rows",
    )(pos, wt, tokens, cot)


def row_block(block, width):
    return pl.BlockSpec((block, width), lambda i: (i, 0))


def piece_specs(n, group):
    half = HALF // n
    shape = (n,) + group[1].shape[1:]
    own = pl.BlockSpec(shape, lambda i: (i, 0, 0))
    low = pl.BlockSpec(shape, lambda i: (jnp.minimum(i, half - 1), 0, 0))
    high = pl.BlockSpec(shape, lambda i: (jnp.maximum(i - half, 0), 0, 0))
    return [own] + [low, high] * 3


def whole(shape):
    return pl.BlockSpec(shape, lambda i: (0,) * len(shape))


def flat(pieces):
    return [x for group in pieces for x in group]


HIDDEN_SOURCES = 16


def hidden_rows(dp, pieces, wg, wu, gathered):
    first = pl.program_id(0) < HALF // HIDDEN_SOURCES
    own, la, lb, ra, rb, fa, fb = pieces
    for shift, x in (
        (0, own[...]),
        (3, jnp.where(first, la[...], lb[...])),
        (1, jnp.where(first, ra[...], rb[...])),
        (2, jnp.where(first, fa[...], fb[...])),
    ):
        q = lax.rem(dp[0] + shift, N_DP)
        gathered[:, :, pl.ds(pl.multiple_of(q * QD, QD), QD)] = x
    rows = own.shape[1]
    x = gathered[...].reshape(HIDDEN_SOURCES * rows, D)
    g = jnp.dot(x, wg[...], preferred_element_type=f32) * scale_in
    u = jnp.dot(x, wu[...], preferred_element_type=f32) * scale_in
    s = 1.0 / (1.0 + jnp.exp(-g))
    slope = u * s * (1.0 + g * (1.0 - s))
    hidden = (g * s * u).astype(bf16)
    shape = (HIDDEN_SOURCES, rows, QF)
    return slope.reshape(shape), hidden.reshape(shape)


def first_hidden_kernel(dp, *refs):
    pieces, (wg, wu, slope_out, h_out, gathered) = refs[:7], refs[7:]
    slope_out[...], h_out[...] = hidden_rows(dp, pieces, wg, wu, gathered)


def last_hidden_kernel(dp, *refs):
    pieces, (wg, wu, before, slope_out, low, high, gathered) = refs[:7], refs[7:]
    slope_out[...], hidden = hidden_rows(dp, pieces, wg, wu, gathered)
    cut = before.shape[1]
    first = pl.program_id(0) < HALF // HIDDEN_SOURCES

    @pl.when(first)
    def _():
        low[:, :cut] = before[...]
        low[:, cut:] = hidden

    @pl.when(jnp.logical_not(first))
    def _():
        high[:, :cut] = before[...]
        high[:, cut:] = hidden


def hidden_call(dp, pieces, wg, wu, before=None):
    n = HIDDEN_SOURCES
    half = HALF // n
    rows = pieces[1].shape[1]
    block = pl.BlockSpec((n, rows, QF), lambda i: (i, 0, 0))
    if before is None:
        extra, specs = (), []
        outs = [jax.ShapeDtypeStruct((SLOTS, rows, QF), bf16)]
        out_specs = [block]
    else:
        extra = (before,)
        specs = [pl.BlockSpec((n,) + before.shape[1:], lambda i: (i, 0, 0))]
        outs = [jax.ShapeDtypeStruct((HALF, CAP, QF), bf16)] * 2
        out_specs = [
            pl.BlockSpec((n, CAP, QF), lambda i: (jnp.minimum(i, half - 1), 0, 0)),
            pl.BlockSpec((n, CAP, QF), lambda i: (jnp.maximum(i - half, 0), 0, 0)),
        ]
    return pl.pallas_call(
        first_hidden_kernel if before is None else last_hidden_kernel,
        grid=(SLOTS // n,),
        out_shape=[jax.ShapeDtypeStruct((SLOTS, rows, QF), f32)] + outs,
        in_specs=[sspec()]
        + piece_specs(n, pieces)
        + [whole((D, QF)), whole((D, QF))]
        + specs,
        out_specs=[block] + out_specs,
        scratch_shapes=[VMEM((n, rows, D), bf16)],
        cost_estimate=cost(4 * SLOTS * rows * D * QF, SLOTS * rows * D * 2 + 8 * D * QF),
        name="hidden0" if before is None else "hidden1",
    )(dp, *pieces, wg, wu, *extra)


PARTIAL_SOURCES = 8


def partial_kernel(dp, x, wd, *outs):
    for k, out in enumerate(outs):
        q = lax.rem(dp[0] + k, N_DP)
        out[...] = lax.dot_general(
            x[:, REST:].reshape(PARTIAL_SOURCES * CAP, QD),
            wd[pl.ds(pl.multiple_of(q * QF, QF), QF), :],
            (((1,), (1,)), ((), ())),
            preferred_element_type=f32,
        ).astype(bf16)


def partial_grads(dp, mixed, wd, part):
    n = PARTIAL_SOURCES
    rows = ROWS // 2
    steps = HALF // n
    return pl.pallas_call(
        partial_kernel,
        grid=(steps,),
        out_shape=[jax.ShapeDtypeStruct((rows, QF), bf16)] * N_DP,
        in_specs=[
            sspec(),
            pl.BlockSpec((n,) + mixed.shape[1:], lambda i: (part * steps + i, 0, 0)),
            whole((FF, QD)),
        ],
        out_specs=[row_block(n * CAP, QF)] * N_DP,
        cost_estimate=cost(2 * rows * QD * FF, 4 << 20),
    )(dp, mixed, wd)


HALF_ROWS = ROWS // 2


def weight_kernel(dp, *refs):
    sums, slope, pieces = refs[:6], refs[6:8], refs[8:22]
    out, x0, x1, parts, slope0, slope1, sems = refs[22:]
    count = len(sums)
    first = [pltpu.make_async_copy(r, parts.at[n], sems.at[n]) for n, r in enumerate(sums)]
    for ref, to in zip(slope, (slope0, slope1)):
        first.append(pltpu.make_async_copy(ref, to, sems.at[count]))
        count += 1
    by_piece = []
    for k in range(N_DP):
        copies = []
        for x, group in ((x0, pieces[:7]), (x1, pieces[7:])):
            if k == 0:
                own = group[0].at[:, pl.ds(0, x.shape[2])]
                copies.append(pltpu.make_async_copy(own, x.at[0], sems.at[count]))
                count += 1
                continue
            for h in range(2):
                to = x.at[k, pl.ds(HALF * h, HALF)]
                copies.append(pltpu.make_async_copy(group[2 * k - 1 + h], to, sems.at[count]))
                count += 1
        by_piece.append(copies)
    for copies in [first] + by_piece:
        for copy in copies:
            copy.start()
    for copy in first:
        copy.wait()
    cut = CHUNKS[0][1]
    gg0, gg1 = [], []
    for h in range(2):
        total = parts[h].astype(f32) + parts[2 + h].astype(f32) + parts[4 + h].astype(f32)
        total = (total * scale_mid).reshape(HALF, CAP, QF)
        at = pl.ds(HALF * h, HALF)
        gg0.append((total[:, :cut] * slope0[at]).astype(bf16).reshape(HALF * cut, QF))
        gg1.append((total[:, cut:] * slope1[at]).astype(bf16).reshape(HALF * (CAP - cut), QF))
    left0 = jnp.concatenate(gg0, axis=0).T
    left1 = jnp.concatenate(gg1, axis=0).T
    for k, shift in enumerate((0, 3, 1, 2)):
        for copy in by_piece[k]:
            copy.wait()
        q = lax.rem(dp[0] + shift, N_DP)
        product = jnp.dot(left0, x0[k].reshape(-1, QD), preferred_element_type=f32)
        product = product + jnp.dot(left1, x1[k].reshape(-1, QD), preferred_element_type=f32)
        to = pl.ds(pl.multiple_of(q * QD, QD), QD)
        out[to, :] = (product * scale_in).astype(bf16).T


def weight_grads(dp, sums, slope, pieces):
    inputs = [*sums, *slope, *flat(pieces)]
    return pl.pallas_call(
        weight_kernel,
        out_shape=jax.ShapeDtypeStruct((D, QF), bf16),
        in_specs=[sspec()] + [pl.BlockSpec(memory_space=pl.ANY)] * len(inputs),
        out_specs=vspec(),
        scratch_shapes=[
            *[VMEM((N_DP, SLOTS, hi - lo, QD), bf16) for lo, hi in CHUNKS],
            VMEM((len(sums), HALF_ROWS, QF), bf16),
            *[VMEM((SLOTS, hi - lo, QF), f32) for lo, hi in CHUNKS],
            pltpu.SemaphoreType.DMA((len(inputs),)),
        ],
        cost_estimate=cost(2 * ROWS * D * QF, ROWS * D * 2 + (4 << 20)),
        name="weight_grads",
    )(dp, *inputs)


def add_kernel(a, b, c, d, low, high):
    low[...] = (a[...].astype(f32) + b[...].astype(f32)).astype(bf16)
    high[...] = (c[...].astype(f32) + d[...].astype(f32)).astype(bf16)


def add_pairs(*arrays):
    return pl.pallas_call(
        add_kernel,
        out_shape=[jax.ShapeDtypeStruct((HALF_ROWS, QF), bf16)] * 2,
        in_specs=[vspec()] * 4,
        out_specs=[vspec()] * 2,
        cost_estimate=cost(2 * HALF_ROWS * QF, 3 << 20),
        name="add_pairs",
    )(*arrays)


OUTPUT_SOURCES = 8


def output_kernel(count, dp, *refs):
    pieces, (wd, out, gathered) = refs[:count], refs[count:]
    first = pl.program_id(0) < HALF // OUTPUT_SOURCES
    for j, shift in zip(range(0, count, 2), (0, 3, 1, 2)):
        q = lax.rem(dp[0] + shift, N_DP)
        to = pl.ds(pl.multiple_of(q * QF, QF), QF)
        gathered[:, :, to] = jnp.where(first, pieces[j][...], pieces[j + 1][...])
    x = gathered[...].reshape(OUTPUT_SOURCES * CAP, FF)
    total = jnp.dot(x, wd[...], preferred_element_type=f32)
    out[...] = (total * scale_mid).astype(bf16)


def outputs_of(dp, pieces, wd):
    n = OUTPUT_SOURCES
    half = HALF // n
    shape = (n, CAP, QF)
    low = pl.BlockSpec(shape, lambda i: (jnp.minimum(i, half - 1), 0, 0))
    high = pl.BlockSpec(shape, lambda i: (jnp.maximum(i - half, 0), 0, 0))
    return pl.pallas_call(
        functools.partial(output_kernel, len(pieces)),
        grid=(SLOTS // n,),
        out_shape=jax.ShapeDtypeStruct((ROWS, QD), bf16),
        in_specs=[sspec()] + [low, high] * N_DP + [whole((FF, QD))],
        out_specs=row_block(n * CAP, QD),
        scratch_shapes=[VMEM((n, CAP, FF), bf16)],
        cost_estimate=cost(2 * ROWS * FF * QD, ROWS * (FF + QD) * 2),
        name="outputs",
    )(dp, *pieces, wd)


def combine(high, low, rows):
    total = None
    for part in (high, low):
        one = lax.dot_general(part, rows, (((0,), (0,)), ((), ())), preferred_element_type=f32)
        total = one if total is None else total + one
    return total.astype(bf16)


UPDATE_ROWS = 16


def update_kernel(plan, placement, grads, gate, first, second, out, total):
    total[...] = jnp.zeros_like(total)
    for s in range(SLOTS):
        total[placement[s]] += grads[s].astype(f32)

    def body(s, carry):
        p = plan[s]
        g = total[placement[p]]
        one = beta_first * first[p].astype(f32) + (1.0 - beta_first) * g
        two = beta_second * second[p].astype(f32) + (1.0 - beta_second) * g * g
        kept = gate[p].astype(f32) * (1.0 - learn_rate * weight_decay)
        out[s, 0] = (kept - learn_rate * one / (jnp.sqrt(two) + epsilon)).astype(bf16)
        out[s, 1] = one.astype(bf16)
        out[s, 2] = two.astype(bf16)
        return carry

    lax.fori_loop(0, SLOTS, body, 0, unroll=4)


def update(plan, placement, grads, states):
    steps = PART // UPDATE_ROWS

    def part(n):
        return pl.BlockSpec((SLOTS, UPDATE_ROWS, QF), lambda i, *_: (0, n * steps + i, 0))

    return pl.pallas_call(
        update_kernel,
        grid_spec=pltpu.PrefetchScalarGridSpec(
            num_scalar_prefetch=2,
            grid=(steps,),
            in_specs=[part(0), part(0), part(1), part(2)],
            out_specs=pl.BlockSpec((SLOTS, 3, UPDATE_ROWS, QF), lambda i, *_: (0, 0, i, 0)),
            scratch_shapes=[VMEM((SLOTS, UPDATE_ROWS, QF), f32)],
        ),
        out_shape=jax.ShapeDtypeStruct((SLOTS, 3, PART, QF), bf16),
        cost_estimate=cost(20 * D * SLOTS * QF // SLOTS, 10 << 20),
        name="update",
    )(plan, placement, grads, states, states, states)


def finish_kernel(moments, *outs):
    for k, out in enumerate(outs):
        out[...] = moments[:, k]


def finish(moments):
    n = 16
    part = pl.BlockSpec((n, PART, QF), lambda i: (i, 0, 0))
    return pl.pallas_call(
        finish_kernel,
        grid=(SLOTS // n,),
        out_shape=[jax.ShapeDtypeStruct((SLOTS, PART, QF), bf16)] * 3,
        in_specs=[pl.BlockSpec((n, 3, PART, QF), lambda i: (i, 0, 0, 0))],
        out_specs=[part] * 3,
        cost_estimate=cost(0, 12 << 20),
        name="finish",
    )(moments)


def exchange(x):
    return lax.all_to_all(x, "expert", split_axis=0, concat_axis=0, tiled=True)


def shift(x, by):
    return lax.ppermute(x, "dp", [(i, (i + by) % N_DP) for i in range(N_DP)])


def ring(low, high):
    la = shift(low, 1)
    rb = shift(high, -1)
    lb = shift(high, 1)
    ra = shift(low, -1)
    fa = shift(la, 1)
    fb = shift(rb, -1)
    return (la, lb, ra, rb, fa, fb)


def device_step(
    tokens,
    cotangent,
    routes,
    route_weight,
    gate_weight,
    up_weight,
    down_weight,
    first_moment,
    second_moment,
    placement,
    migration_plan,
):
    index = lax.axis_index("expert").astype(jnp.int32)[None]
    dp = lax.axis_index("dp").astype(jnp.int32)[None]
    wg, wu, wd = gate_weight[0], up_weight[0], down_weight[0]
    first_rows, pos, wt = select_rows(index, placement, routes, route_weight, tokens)
    sent, weight_high, weight_low = mixed_rows(pos, wt, tokens, cotangent)
    got = exchange(first_rows)
    mixed = exchange(sent)
    packed = jnp.concatenate(
        [x[0].reshape(SLOTS, PART, QF) for x in (gate_weight, first_moment, second_moment)],
        axis=1,
    )
    states = exchange(packed)
    pieces = [
        (got, *ring(got[:HALF], got[HALF:])),
        (mixed, *ring(mixed[:HALF, :REST], mixed[HALF:, :REST])),
    ]
    slope0, before = hidden_call(dp, pieces[0], wg, wu)
    slope1, *h = hidden_call(dp, pieces[1], wg, wu, before)
    low = partial_grads(dp, mixed, wd, 0)
    high = partial_grads(dp, mixed, wd, 1)
    far_low = shift(low[2], 1)
    far_high = shift(high[2], -1)
    near_low = shift(low[3], -1)
    near_high = shift(high[1], 1)
    pair_low, pair_high = add_pairs(low[1], far_low, high[3], far_high)
    pair_low = shift(pair_low, 1)
    pair_high = shift(pair_high, -1)
    sums = (low[0], high[0], near_low, near_high, pair_low, pair_high)
    wgrad = weight_grads(dp, sums, (slope0, slope1), pieces)
    got_wgrad = exchange(wgrad.reshape(SLOTS, PART, QF))
    moments = exchange(update(migration_plan, placement, got_wgrad, states))
    out = outputs_of(dp, (*h, *ring(*h)), wd)
    returned = exchange(out.reshape(SLOTS, CAP, QD)).reshape(ROWS, QD)
    layer_output = combine(weight_high, weight_low, returned)
    results = finish(moments)
    return (layer_output,) + tuple(r.reshape(1, D, QF) for r in results)


def solution(mesh):
    placed = (
        P("expert", "dp"),
        P("expert", "dp"),
        P("expert", None),
        P("expert", None),
        P("expert", None, "dp"),
        P("expert", None, "dp"),
        P("expert", None, "dp"),
        P("expert", None, "dp"),
        P("expert", None, "dp"),
        P(),
        P(),
    )
    return jax.shard_map(
        device_step,
        mesh=mesh,
        in_specs=placed,
        out_specs=(
            P("expert", "dp"),
            P("expert", None, "dp"),
            P("expert", None, "dp"),
            P("expert", None, "dp"),
        ),
        check_vma=False,
    )
```

```python
import functools
import math

import jax
import jax.numpy as jnp
from jax import lax
from jax.experimental import pallas as pl
from jax.experimental.pallas import tpu as pltpu
from jax.sharding import PartitionSpec as P


D = 3584
FF = 1024
N_DP = 4
SLOTS = 32
CAP = 48
TOK = 128
QD = D // N_DP
QF = FF // N_DP
PART = D // SLOTS
CHUNKS = ((0, 16), (16, 48))
ROWS = SLOTS * CAP
HALF = SLOTS // 2

beta_first = 0.9
beta_second = 0.95
learn_rate = 0.02
weight_decay = 0.1
epsilon = 1e-08
scale_in = 1.0 / math.sqrt(D)
scale_mid = 1.0 / math.sqrt(FF)


f32 = jnp.float32
bf16 = jnp.bfloat16
VMEM = pltpu.VMEM
SMEM = pltpu.SMEM


def vspec():
    return pl.BlockSpec(memory_space=VMEM)


def sspec():
    return pl.BlockSpec(memory_space=SMEM)


def cost(flops, nbytes):
    return pl.CostEstimate(flops=flops, transcendentals=0, bytes_accessed=nbytes)


def select_kernel(index, place, routes, weights, tokens, out, pos_out, wt_out, sel):
    me = index[0].astype(f32)
    a = lax.broadcasted_iota(jnp.int32, (SLOTS, SLOTS), 0)
    b = lax.broadcasted_iota(jnp.int32, (SLOTS, SLOTS), 1)
    row = place[...].astype(f32)
    col = jnp.sum(jnp.where(a == b, row, 0.0), axis=1, keepdims=True)
    same = jnp.where(jnp.abs(col - row) < 0.5, 1.0, 0.0)
    copies = jnp.sum(same, axis=1, keepdims=True)
    rank = jnp.sum(jnp.where(b < a, same, 0.0), axis=1, keepdims=True)
    turn = me - copies * jnp.floor((me + 0.5) / copies)
    active = jnp.abs(rank - turn) < 0.5
    hit = jnp.zeros((SLOTS, TOK), f32)
    wt = jnp.zeros((SLOTS, TOK), f32)
    for k in range(routes.shape[0]):
        match = (jnp.abs(routes[k : k + 1, :].astype(f32) - col) < 0.5) & active
        hit = hit + jnp.where(match, 1.0, 0.0)
        wt = wt + jnp.where(match, weights[k : k + 1, :], 0.0)
    t0 = lax.broadcasted_iota(jnp.int32, (TOK, TOK), 0)
    t1 = lax.broadcasted_iota(jnp.int32, (TOK, TOK), 1)
    before = jnp.where(t0 < t1, 1.0, 0.0).astype(bf16)
    pos = jnp.dot(hit.astype(bf16), before, preferred_element_type=f32)
    pos = jnp.where(hit > 0.5, pos, -1.0)
    pos_out[...] = pos
    wt_out[...] = wt
    mark_rows(pos, wt, CHUNKS[0], sel, None)
    spread_rows(CHUNKS[0], sel, tokens, out)


def mark_rows(pos, wt, chunk, sel, selw):
    lo, hi = chunk
    want = (lax.broadcasted_iota(jnp.int32, (hi - lo, TOK), 0) + lo).astype(f32)
    for j in range(SLOTS):
        chosen = jnp.abs(pos[j : j + 1, :] - want) < 0.5
        if sel is not None:
            sel[j] = jnp.where(chosen, 1.0, 0.0).astype(bf16)
        if selw is not None:
            selw[j] = jnp.where(chosen, wt[j : j + 1, :], 0.0)


def spread_rows(chunk, sel, values, out):
    rows = chunk[1] - chunk[0]
    group = 256 // rows
    for j in range(0, SLOTS, group):
        picks = sel[j : j + group].reshape(group * rows, TOK)
        got = jnp.dot(picks, values[...], preferred_element_type=f32).astype(bf16)
        out[j : j + group] = got.reshape(group, rows, QD)


def select_rows(index, placement, routes, weights, tokens):
    rows = CHUNKS[0][1]
    return pl.pallas_call(
        select_kernel,
        out_shape=[
            jax.ShapeDtypeStruct((SLOTS, rows, QD), bf16),
            jax.ShapeDtypeStruct((SLOTS, TOK), f32),
            jax.ShapeDtypeStruct((SLOTS, TOK), f32),
        ],
        in_specs=[sspec()] + [vspec()] * 4,
        out_specs=[vspec()] * 3,
        scratch_shapes=[VMEM((SLOTS, rows, TOK), bf16)],
        cost_estimate=cost(2 * ROWS * TOK * QD // 3, 2 << 20),
        name="select_rows",
    )(index, placement[None, :], routes.T, weights.T, tokens)


def rest_kernel(pos_in, tokens, out, sel):
    pos = pos_in[...]
    mark_rows(pos, None, CHUNKS[1], sel, None)
    spread_rows(CHUNKS[1], sel, tokens, out)


def rest_rows(pos, tokens):
    lo, hi = CHUNKS[1]
    return pl.pallas_call(
        rest_kernel,
        out_shape=jax.ShapeDtypeStruct((SLOTS, hi - lo, QD), bf16),
        in_specs=[vspec()] * 2,
        out_specs=vspec(),
        scratch_shapes=[VMEM((SLOTS, hi - lo, TOK), bf16)],
        cost_estimate=cost(2 * ROWS * TOK * QD, 4 << 20),
        name="rest_rows",
    )(pos, tokens)


def scale_kernel(pos_in, wt_in, cot, out, high_out, low_out, selw):
    mark_rows(pos_in[...], wt_in[...], (0, CAP), None, selw)
    group = 8
    for j in range(0, SLOTS, group):
        w = selw[j : j + group].reshape(group * CAP, TOK)
        picks = jnp.where(w != 0.0, 1.0, 0.0).astype(bf16)
        picked = jnp.dot(picks, cot[...], preferred_element_type=f32)
        rows = pl.ds(j * CAP, group * CAP)
        out[rows, :] = (jnp.sum(w, axis=1, keepdims=True) * picked).astype(bf16)
        high = w.astype(bf16)
        high_out[rows, :] = high
        low_out[rows, :] = (w - high.astype(f32)).astype(bf16)


def scale_rows(pos, wt, cot):
    return pl.pallas_call(
        scale_kernel,
        out_shape=[
            jax.ShapeDtypeStruct((ROWS, QD), bf16),
            jax.ShapeDtypeStruct((ROWS, TOK), bf16),
            jax.ShapeDtypeStruct((ROWS, TOK), bf16),
        ],
        in_specs=[vspec()] * 3,
        out_specs=[vspec()] * 3,
        scratch_shapes=[VMEM((SLOTS, CAP, TOK), f32)],
        cost_estimate=cost(2 * ROWS * TOK * QD, 4 << 20),
        name="scale_rows",
    )(pos, wt, cot)


def row_block(block, width):
    return pl.BlockSpec((block, width), lambda i: (i, 0))


def piece_specs(n, group):
    half = HALF // n
    shape = (n,) + group[0].shape[1:]
    own = pl.BlockSpec(shape, lambda i: (i, 0, 0))
    low = pl.BlockSpec(shape, lambda i: (jnp.minimum(i, half - 1), 0, 0))
    high = pl.BlockSpec(shape, lambda i: (jnp.maximum(i - half, 0), 0, 0))
    return [own] + [low, high] * 3


def whole(shape):
    return pl.BlockSpec(shape, lambda i: (0,) * len(shape))


def flat(pieces):
    return [x for group in pieces for x in group]


HIDDEN_SOURCES = 16


def hidden_rows(dp, pieces, wg, wu, gathered):
    first = pl.program_id(0) < HALF // HIDDEN_SOURCES
    own, la, lb, ra, rb, fa, fb = pieces
    for shift, x in (
        (0, own[...]),
        (3, jnp.where(first, la[...], lb[...])),
        (1, jnp.where(first, ra[...], rb[...])),
        (2, jnp.where(first, fa[...], fb[...])),
    ):
        q = lax.rem(dp[0] + shift, N_DP)
        gathered[:, :, pl.ds(pl.multiple_of(q * QD, QD), QD)] = x
    rows = own.shape[1]
    x = gathered[...].reshape(HIDDEN_SOURCES * rows, D)
    g = jnp.dot(x, wg[...], preferred_element_type=f32) * scale_in
    u = jnp.dot(x, wu[...], preferred_element_type=f32) * scale_in
    s = 1.0 / (1.0 + jnp.exp(-g))
    slope = u * s * (1.0 + g * (1.0 - s))
    hidden = (g * s * u).astype(bf16)
    shape = (HIDDEN_SOURCES, rows, QF)
    return slope.reshape(shape), hidden.reshape(shape)


def first_hidden_kernel(dp, *refs):
    pieces, (wg, wu, slope_out, h_out, gathered) = refs[:7], refs[7:]
    slope_out[...], h_out[...] = hidden_rows(dp, pieces, wg, wu, gathered)


def last_hidden_kernel(dp, *refs):
    pieces, (wg, wu, before, slope_out, low, high, gathered) = refs[:7], refs[7:]
    slope_out[...], hidden = hidden_rows(dp, pieces, wg, wu, gathered)
    cut = before.shape[1]
    first = pl.program_id(0) < HALF // HIDDEN_SOURCES

    @pl.when(first)
    def _():
        low[:, :cut] = before[...]
        low[:, cut:] = hidden

    @pl.when(jnp.logical_not(first))
    def _():
        high[:, :cut] = before[...]
        high[:, cut:] = hidden


def hidden_call(dp, pieces, wg, wu, before=None):
    n = HIDDEN_SOURCES
    half = HALF // n
    rows = pieces[0].shape[1]
    block = pl.BlockSpec((n, rows, QF), lambda i: (i, 0, 0))
    if before is None:
        extra, specs = (), []
        outs = [jax.ShapeDtypeStruct((SLOTS, rows, QF), bf16)]
        out_specs = [block]
    else:
        extra = (before,)
        specs = [pl.BlockSpec((n,) + before.shape[1:], lambda i: (i, 0, 0))]
        outs = [jax.ShapeDtypeStruct((HALF, CAP, QF), bf16)] * 2
        out_specs = [
            pl.BlockSpec((n, CAP, QF), lambda i: (jnp.minimum(i, half - 1), 0, 0)),
            pl.BlockSpec((n, CAP, QF), lambda i: (jnp.maximum(i - half, 0), 0, 0)),
        ]
    return pl.pallas_call(
        first_hidden_kernel if before is None else last_hidden_kernel,
        grid=(SLOTS // n,),
        out_shape=[jax.ShapeDtypeStruct((SLOTS, rows, QF), f32)] + outs,
        in_specs=[sspec()]
        + piece_specs(n, pieces)
        + [whole((D, QF)), whole((D, QF))]
        + specs,
        out_specs=[block] + out_specs,
        scratch_shapes=[VMEM((n, rows, D), bf16)],
        cost_estimate=cost(4 * SLOTS * rows * D * QF, SLOTS * rows * D * 2 + 8 * D * QF),
        name="hidden0" if before is None else "hidden1",
    )(dp, *pieces, wg, wu, *extra)


PARTIAL_BLOCK = 384


def partial_kernel(dp, x, wd, *outs):
    for k, out in enumerate(outs):
        q = lax.rem(dp[0] + k, N_DP)
        out[...] = lax.dot_general(
            x[...],
            wd[pl.ds(pl.multiple_of(q * QF, QF), QF), :],
            (((1,), (1,)), ((), ())),
            preferred_element_type=f32,
        ).astype(bf16)


def partial_grads(dp, x, wd, part):
    block = PARTIAL_BLOCK
    rows = ROWS // 2
    steps = rows // block
    return pl.pallas_call(
        partial_kernel,
        grid=(steps,),
        out_shape=[jax.ShapeDtypeStruct((rows, QF), bf16)] * N_DP,
        in_specs=[
            sspec(),
            pl.BlockSpec((block, QD), lambda i: (part * steps + i, 0)),
            whole((FF, QD)),
        ],
        out_specs=[row_block(block, QF)] * N_DP,
        cost_estimate=cost(2 * rows * QD * FF, 4 << 20),
    )(dp, x, wd)


HALF_ROWS = ROWS // 2


def weight_kernel(dp, *refs):
    sums, slope, pieces = refs[:6], refs[6:8], refs[8:22]
    out, x0, x1, parts, slope0, slope1, sems = refs[22:]
    count = len(sums)
    first = [pltpu.make_async_copy(r, parts.at[n], sems.at[n]) for n, r in enumerate(sums)]
    for ref, to in zip(slope, (slope0, slope1)):
        first.append(pltpu.make_async_copy(ref, to, sems.at[count]))
        count += 1
    by_piece = []
    for k in range(N_DP):
        copies = []
        for x, group in ((x0, pieces[:7]), (x1, pieces[7:])):
            if k == 0:
                copies.append(pltpu.make_async_copy(group[0], x.at[0], sems.at[count]))
                count += 1
                continue
            for h in range(2):
                to = x.at[k, pl.ds(HALF * h, HALF)]
                copies.append(pltpu.make_async_copy(group[2 * k - 1 + h], to, sems.at[count]))
                count += 1
        by_piece.append(copies)
    for copies in [first] + by_piece:
        for copy in copies:
            copy.start()
    for copy in first:
        copy.wait()
    cut = CHUNKS[0][1]
    gg0, gg1 = [], []
    for h in range(2):
        total = parts[h].astype(f32) + parts[2 + h].astype(f32) + parts[4 + h].astype(f32)
        total = (total * scale_mid).reshape(HALF, CAP, QF)
        at = pl.ds(HALF * h, HALF)
        gg0.append((total[:, :cut] * slope0[at]).astype(bf16).reshape(HALF * cut, QF))
        gg1.append((total[:, cut:] * slope1[at]).astype(bf16).reshape(HALF * (CAP - cut), QF))
    left0 = jnp.concatenate(gg0, axis=0).T
    left1 = jnp.concatenate(gg1, axis=0).T
    for k, shift in enumerate((0, 3, 1, 2)):
        for copy in by_piece[k]:
            copy.wait()
        q = lax.rem(dp[0] + shift, N_DP)
        product = jnp.dot(left0, x0[k].reshape(-1, QD), preferred_element_type=f32)
        product = product + jnp.dot(left1, x1[k].reshape(-1, QD), preferred_element_type=f32)
        to = pl.ds(pl.multiple_of(q * QD, QD), QD)
        out[to, :] = (product * scale_in).astype(bf16).T


def weight_grads(dp, sums, slope, pieces):
    inputs = [*sums, *slope, *flat(pieces)]
    return pl.pallas_call(
        weight_kernel,
        out_shape=jax.ShapeDtypeStruct((D, QF), bf16),
        in_specs=[sspec()] + [pl.BlockSpec(memory_space=pl.ANY)] * len(inputs),
        out_specs=vspec(),
        scratch_shapes=[
            *[VMEM((N_DP, SLOTS, hi - lo, QD), bf16) for lo, hi in CHUNKS],
            VMEM((len(sums), HALF_ROWS, QF), bf16),
            *[VMEM((SLOTS, hi - lo, QF), f32) for lo, hi in CHUNKS],
            pltpu.SemaphoreType.DMA((len(inputs),)),
        ],
        cost_estimate=cost(2 * ROWS * D * QF, ROWS * D * 2 + (4 << 20)),
        name="weight_grads",
    )(dp, *inputs)


def add_kernel(a, b, c, d, low, high):
    low[...] = (a[...].astype(f32) + b[...].astype(f32)).astype(bf16)
    high[...] = (c[...].astype(f32) + d[...].astype(f32)).astype(bf16)


def add_pairs(*arrays):
    return pl.pallas_call(
        add_kernel,
        out_shape=[jax.ShapeDtypeStruct((HALF_ROWS, QF), bf16)] * 2,
        in_specs=[vspec()] * 4,
        out_specs=[vspec()] * 2,
        cost_estimate=cost(2 * HALF_ROWS * QF, 3 << 20),
        name="add_pairs",
    )(*arrays)


OUTPUT_SOURCES = 8


def output_kernel(count, dp, *refs):
    pieces, (wd, out, gathered) = refs[:count], refs[count:]
    first = pl.program_id(0) < HALF // OUTPUT_SOURCES
    for j, shift in zip(range(0, count, 2), (0, 3, 1, 2)):
        q = lax.rem(dp[0] + shift, N_DP)
        to = pl.ds(pl.multiple_of(q * QF, QF), QF)
        gathered[:, :, to] = jnp.where(first, pieces[j][...], pieces[j + 1][...])
    x = gathered[...].reshape(OUTPUT_SOURCES * CAP, FF)
    total = jnp.dot(x, wd[...], preferred_element_type=f32)
    out[...] = (total * scale_mid).astype(bf16)


def outputs_of(dp, pieces, wd):
    n = OUTPUT_SOURCES
    half = HALF // n
    shape = (n, CAP, QF)
    low = pl.BlockSpec(shape, lambda i: (jnp.minimum(i, half - 1), 0, 0))
    high = pl.BlockSpec(shape, lambda i: (jnp.maximum(i - half, 0), 0, 0))
    return pl.pallas_call(
        functools.partial(output_kernel, len(pieces)),
        grid=(SLOTS // n,),
        out_shape=jax.ShapeDtypeStruct((ROWS, QD), bf16),
        in_specs=[sspec()] + [low, high] * N_DP + [whole((FF, QD))],
        out_specs=row_block(n * CAP, QD),
        scratch_shapes=[VMEM((n, CAP, FF), bf16)],
        cost_estimate=cost(2 * ROWS * FF * QD, ROWS * (FF + QD) * 2),
        name="outputs",
    )(dp, *pieces, wd)


def combine(high, low, rows):
    total = None
    for part in (high, low):
        one = lax.dot_general(part, rows, (((0,), (0,)), ((), ())), preferred_element_type=f32)
        total = one if total is None else total + one
    return total.astype(bf16)


UPDATE_ROWS = 16


def update_kernel(plan, placement, grads, gate, first, second, out, total):
    total[...] = jnp.zeros_like(total)
    for s in range(SLOTS):
        total[placement[s]] += grads[s].astype(f32)

    def body(s, carry):
        p = plan[s]
        g = total[placement[p]]
        one = beta_first * first[p].astype(f32) + (1.0 - beta_first) * g
        two = beta_second * second[p].astype(f32) + (1.0 - beta_second) * g * g
        kept = gate[p].astype(f32) * (1.0 - learn_rate * weight_decay)
        out[s, 0] = (kept - learn_rate * one / (jnp.sqrt(two) + epsilon)).astype(bf16)
        out[s, 1] = one.astype(bf16)
        out[s, 2] = two.astype(bf16)
        return carry

    lax.fori_loop(0, SLOTS, body, 0, unroll=4)


def update(plan, placement, grads, states):
    steps = PART // UPDATE_ROWS

    def part(n):
        return pl.BlockSpec((SLOTS, UPDATE_ROWS, QF), lambda i, *_: (0, n * steps + i, 0))

    return pl.pallas_call(
        update_kernel,
        grid_spec=pltpu.PrefetchScalarGridSpec(
            num_scalar_prefetch=2,
            grid=(steps,),
            in_specs=[part(0), part(0), part(1), part(2)],
            out_specs=pl.BlockSpec((SLOTS, 3, UPDATE_ROWS, QF), lambda i, *_: (0, 0, i, 0)),
            scratch_shapes=[VMEM((SLOTS, UPDATE_ROWS, QF), f32)],
        ),
        out_shape=jax.ShapeDtypeStruct((SLOTS, 3, PART, QF), bf16),
        cost_estimate=cost(20 * D * SLOTS * QF // SLOTS, 10 << 20),
        name="update",
    )(plan, placement, grads, states, states, states)


def finish_kernel(moments, *outs):
    for k, out in enumerate(outs):
        out[...] = moments[:, k]


def finish(moments):
    n = 16
    part = pl.BlockSpec((n, PART, QF), lambda i: (i, 0, 0))
    return pl.pallas_call(
        finish_kernel,
        grid=(SLOTS // n,),
        out_shape=[jax.ShapeDtypeStruct((SLOTS, PART, QF), bf16)] * 3,
        in_specs=[pl.BlockSpec((n, 3, PART, QF), lambda i: (i, 0, 0, 0))],
        out_specs=[part] * 3,
        cost_estimate=cost(0, 12 << 20),
        name="finish",
    )(moments)


def exchange(x):
    return lax.all_to_all(x, "expert", split_axis=0, concat_axis=0, tiled=True)


def shift(x, by):
    return lax.ppermute(x, "dp", [(i, (i + by) % N_DP) for i in range(N_DP)])


def ring(low, high):
    la = shift(low, 1)
    rb = shift(high, -1)
    lb = shift(high, 1)
    ra = shift(low, -1)
    fa = shift(la, 1)
    fb = shift(rb, -1)
    return (la, lb, ra, rb, fa, fb)


def device_step(
    tokens,
    cotangent,
    routes,
    route_weight,
    gate_weight,
    up_weight,
    down_weight,
    first_moment,
    second_moment,
    placement,
    migration_plan,
):
    index = lax.axis_index("expert").astype(jnp.int32)[None]
    dp = lax.axis_index("dp").astype(jnp.int32)[None]
    wg, wu, wd = gate_weight[0], up_weight[0], down_weight[0]
    first_rows, pos, wt = select_rows(index, placement, routes, route_weight, tokens)
    rows = (first_rows, rest_rows(pos, tokens))
    got = [exchange(x) for x in rows]
    sent_grads, weight_high, weight_low = scale_rows(pos, wt, cotangent)
    got_grads = exchange(sent_grads.reshape(SLOTS, CAP, QD)).reshape(ROWS, QD)
    packed = jnp.concatenate(
        [x[0].reshape(SLOTS, PART, QF) for x in (gate_weight, first_moment, second_moment)],
        axis=1,
    )
    states = exchange(packed)
    pieces = [(x, *ring(x[:HALF], x[HALF:])) for x in got]
    slope0, before = hidden_call(dp, pieces[0], wg, wu)
    slope1, *h = hidden_call(dp, pieces[1], wg, wu, before)
    low = partial_grads(dp, got_grads, wd, 0)
    high = partial_grads(dp, got_grads, wd, 1)
    far_low = shift(low[2], 1)
    far_high = shift(high[2], -1)
    near_low = shift(low[3], -1)
    near_high = shift(high[1], 1)
    pair_low, pair_high = add_pairs(low[1], far_low, high[3], far_high)
    pair_low = shift(pair_low, 1)
    pair_high = shift(pair_high, -1)
    sums = (low[0], high[0], near_low, near_high, pair_low, pair_high)
    wgrad = weight_grads(dp, sums, (slope0, slope1), pieces)
    got_wgrad = exchange(wgrad.reshape(SLOTS, PART, QF))
    moments = exchange(update(migration_plan, placement, got_wgrad, states))
    out = outputs_of(dp, (*h, *ring(*h)), wd)
    returned = exchange(out.reshape(SLOTS, CAP, QD)).reshape(ROWS, QD)
    layer_output = combine(weight_high, weight_low, returned)
    results = finish(moments)
    return (layer_output,) + tuple(r.reshape(1, D, QF) for r in results)


def solution(mesh):
    placed = (
        P("expert", "dp"),
        P("expert", "dp"),
        P("expert", None),
        P("expert", None),
        P("expert", None, "dp"),
        P("expert", None, "dp"),
        P("expert", None, "dp"),
        P("expert", None, "dp"),
        P("expert", None, "dp"),
        P(),
        P(),
    )
    return jax.shard_map(
        device_step,
        mesh=mesh,
        in_specs=placed,
        out_specs=(
            P("expert", "dp"),
            P("expert", None, "dp"),
            P("expert", None, "dp"),
            P("expert", None, "dp"),
        ),
        check_vma=False,
    )
```
